256 devices in a mesh: dp: 2 (over core), tvoc: 16 (over x, y), svoc: 8 (over z).
Axes of the slice: x: 4, y: 4, z: 8, core: 2. Of those that a mesh axis runs over, the one named last changes fastest.
Arguments:
- teacher_probs: bfloat16 [256, 81920], P('dp', 'tvoc'), may hold values from 0 to 1, as said below
- block_values: bfloat16 [16, 8, 24, 128, 128], P('tvoc', 'svoc'), may hold values from 0.0099487305 to 1
- block_index: int32 [16, 8, 24, 2], P('tvoc', 'svoc'), may hold values from 0 to 63, as said below
- block_count: int32 [16, 8], P('tvoc', 'svoc'), may hold values from 17 to 24, as said below
- hidden: bfloat16 [256, 3072], P('dp'), may hold values from -48 to 48
- student_weight: bfloat16 [3072, 65536], P(None, ('tvoc', 'svoc')), may hold values from -0.15 to 0.15
Outputs:
- divergence: float32 [256], P('dp')
- grad_weight: bfloat16 [3072, 65536], P('dp', ('tvoc', 'svoc'))
- grad_hidden: float32 [256, 3072], P('dp', ('tvoc', 'svoc'))
The draws below stay inside these ranges and needn't reach their ends.
Inputs may be any that keep to these rules, and one draw needn't show every extreme that they name: `teacher_probs`: each row sums to one and every entry is positive. `block_index`: entry [i, j, s, 0] is a teacher block of shard i, entry [i, j, s, 1] is c as in the reference program. The live slots of one device name at most 2 distinct c with the same c // 4, and some value of c // 4 reaches 2 on every device. Several live slots may name the same c, with the same or another teacher block. `block_count`: the live slots are the first ones; some device has all 24 live.
All inputs are finite; a program needn't handle non-finite values.
Results may differ from the reference program's by a relative error of at most 0.013.
Values may be sent and summed in bfloat16 or wider, within the bound.
No kernel may reach another device: no remote copies, remote signals or barrier semaphores. Data moves between devices by JAX's collectives and lax.ppermute only.
A program may use at most 64 MiB of HBM per device.

```python
import math
import jax
import jax.numpy as jnp
from jax import lax

D = 3072
BLK = 128
TVB_DEV = 40
SVB_DEV = 4
SLOTS = 24
CAP = 2
TOKENS = 256
TEACHER_VOCAB = 81920
STUDENT_VOCAB = 65536
N_TVOC = 16
N_SVOC = 8


weight_limit = 0.1484375


def index_plan(key):
    base_key = jax.random.fold_in(key, 11)
    lowest = N_TVOC * (CAP - 1) + 1
    spread = SLOTS - lowest
    pair_total = N_TVOC * CAP

    def draw_device(device_key):
        pick_key, order_key, row_key, count_key, source_key, coin_key = jax.random.split(device_key, 6)
        pick_keys = jax.random.split(pick_key, N_TVOC)
        chosen = jax.vmap(lambda single_key: jax.random.permutation(single_key, SVB_DEV)[:CAP])(pick_keys)
        order = jax.random.permutation(order_key, pair_total)
        slot_range = jnp.arange(SLOTS, dtype=jnp.int32)
        fresh = order[slot_range % pair_total]
        source = jax.random.randint(source_key, (SLOTS,), 0, lowest)
        coin = jax.random.randint(coin_key, (SLOTS,), 0, 2) == 1
        pairing = jnp.where((slot_range >= lowest) & coin, order[source], fresh)
        owner = pairing // CAP
        within = pairing % CAP
        columns = owner * SVB_DEV + chosen[owner, within]
        teacher_rows = jax.random.randint(row_key, (SLOTS,), 0, TVB_DEV)
        offset = jax.random.randint(count_key, (), 0, spread + 1)
        count = SLOTS - offset * offset // max(spread, 1)
        return (jnp.stack([teacher_rows, columns], axis=-1).astype(jnp.int32), count.astype(jnp.int32))
    device_keys = jax.random.split(base_key, N_TVOC * N_SVOC)
    indices, counts = jax.vmap(draw_device)(device_keys)
    fullest = jax.random.randint(jax.random.fold_in(base_key, 5), (), 0, N_TVOC * N_SVOC)
    counts = jnp.where(jnp.arange(N_TVOC * N_SVOC) == fullest, SLOTS, counts)
    return (indices.reshape(N_TVOC, N_SVOC, SLOTS, 2), counts.reshape(N_TVOC, N_SVOC).astype(jnp.int32))


def draw_block_index(key, part):
    return index_plan(key)[0]


def draw_block_count(key, part):
    return index_plan(key)[1]


def weight_columns(key, chosen):
    column_key = jax.random.fold_in(key, 31)

    def single(column):
        return jax.random.normal(jax.random.fold_in(column_key, column), (D,), jnp.float32)
    return jax.vmap(single)(chosen) / math.sqrt(D)


def draw_student_weight(key, part):
    columns = weight_columns(key, jnp.arange(STUDENT_VOCAB, dtype=jnp.int32))
    return jnp.clip(columns.T, -weight_limit, weight_limit).astype(jnp.bfloat16)


def draw_hidden(key, part):
    base_key = jax.random.fold_in(key, 41)
    noise_key = jax.random.fold_in(base_key, 0)
    states = jax.random.normal(noise_key, (TOKENS, D), jnp.float32)
    return jnp.clip(states, -48.0, 48.0).astype(jnp.bfloat16)


def draw_teacher_probs(key, part):
    noise_key, column_key = jax.random.split(jax.random.fold_in(key, 21), 2)
    shape = (TOKENS, TEACHER_VOCAB)
    column_bias = jax.random.normal(column_key, (1, TEACHER_VOCAB), jnp.float32)
    scores = 1.5 * jax.random.normal(noise_key, shape, jnp.float32) + column_bias
    return jax.nn.softmax(scores, axis=-1).astype(jnp.bfloat16)


def levels(stream_key, shape, cuts, least, top_value):
    level = 1.0
    for position, parts in cuts:
        steps = jax.random.uniform(jax.random.fold_in(jax.random.fold_in(stream_key, 6), position), (parts,), jnp.float32, least / len(cuts), top_value / len(cuts))
        level = level * jnp.repeat(jnp.exp(steps), shape[position] // parts).reshape((-1,) + (1,) * (len(shape) - 1 - position))
    return level


def setup_inputs(seed: int = 0) -> dict:
    streams_of = jax.random.split(jax.random.key(seed), 7)
    return {
        "teacher_probs": draw_teacher_probs(jax.random.fold_in(streams_of[6], 71), 0),
        "block_values": jnp.clip(jnp.exp(math.log(1.0) - 4.61031033 * jax.random.uniform(streams_of[1], (N_TVOC, N_SVOC, SLOTS, BLK, BLK), jnp.float32) ** levels(streams_of[1], (N_TVOC, N_SVOC, SLOTS, BLK, BLK), ((0, 16), (1, 8)), -0.2, 0.2)), 0.0099487305, 1.0).astype(jnp.bfloat16),
        "block_index": draw_block_index(jax.random.fold_in(streams_of[6], 71), 0),
        "block_count": draw_block_count(jax.random.fold_in(streams_of[6], 71), 0),
        "hidden": draw_hidden(jax.random.fold_in(streams_of[6], 71), 0),
        "student_weight": draw_student_weight(jax.random.fold_in(streams_of[6], 71), 0),
    }


def reference(teacher_probs, block_values, block_index, block_count, hidden, student_weight):
    loss_scale = 128.0
    owned = N_TVOC * SVB_DEV
    shard_width = SVB_DEV * BLK

    def device_partial(teacher_shard, student_shard):
        shard_probs = lax.dynamic_slice_in_dim(teacher_probs, teacher_shard * (TVB_DEV * BLK), TVB_DEV * BLK, 1)
        shard_probs = shard_probs.reshape(TOKENS, TVB_DEV, BLK)
        indices = block_index[teacher_shard, student_shard]
        entries = block_values[teacher_shard, student_shard]
        occupied = (jnp.arange(SLOTS, dtype=jnp.int32) < block_count[teacher_shard, student_shard]).astype(jnp.float32)
        picked = jnp.take(shard_probs, indices[:, 0], axis=1)
        mapped = jnp.einsum('tsk,skc->stc', picked.astype(jnp.float32), entries.astype(jnp.float32))
        mapped = mapped * occupied[:, None, None]
        summed = jnp.zeros((owned, TOKENS, BLK), jnp.float32).at[indices[:, 1]].add(mapped)
        rounded = lax.optimization_barrier(summed.astype(jnp.bfloat16))
        return jnp.transpose(rounded.astype(jnp.float32), (1, 0, 2))

    def per_student(student_shard):

        def accumulate(running, teacher_shard):
            return (running + device_partial(teacher_shard, student_shard), None)
        running, _ = lax.scan(accumulate, jnp.zeros((TOKENS, owned, BLK), jnp.float32), jnp.arange(N_TVOC, dtype=jnp.int32))
        return running
    stacked = lax.map(per_student, jnp.arange(N_SVOC, dtype=jnp.int32))
    stacked = stacked.reshape(N_SVOC, TOKENS, N_TVOC, shard_width)
    teacher_mass = jnp.transpose(stacked, (1, 2, 0, 3)).reshape(TOKENS, STUDENT_VOCAB)
    logits = jnp.dot(hidden.astype(jnp.float32), student_weight.astype(jnp.float32), preferred_element_type=jnp.float32)
    largest = jnp.max(logits, axis=1)
    shifted = jnp.exp(logits - largest[:, None])
    total = jnp.sum(shifted, axis=1)
    mass_sum = jnp.sum(teacher_mass, axis=1)
    target = teacher_mass / mass_sum[:, None]
    positive = target > 0
    log_target = jnp.log(jnp.where(positive, target, 1.0))
    terms = jnp.where(positive, target * log_target, 0.0) - target * (logits - largest[:, None] - jnp.log(total)[:, None])
    divergence = jnp.sum(terms, axis=1)
    logit_grad = (loss_scale * (shifted / total[:, None] - target)).astype(jnp.bfloat16)
    grad_weight = jnp.dot(hidden.T.astype(jnp.float32), logit_grad.astype(jnp.float32), preferred_element_type=jnp.float32).astype(jnp.bfloat16)
    grad_hidden = jnp.dot(logit_grad.astype(jnp.float32), student_weight.T.astype(jnp.float32), preferred_element_type=jnp.float32)
    return (divergence, grad_weight, grad_hidden)
```

```python
import jax
import jax.numpy as jnp
from jax import lax
from jax.experimental import pallas as pl
from jax.experimental.pallas import tpu as pltpu
from jax.sharding import Mesh
from jax.sharding import PartitionSpec as P

CAP = 2
TVOC = ("tvoc_0", "tvoc_1")
TVOC_SVOC = ("tvoc_0", "tvoc_1", "svoc")
LOSS_SCALE = 128.0
F32 = jnp.float32
BF16 = jnp.bfloat16
EXTRA = 8


def vmem():
    return pl.BlockSpec(memory_space=pltpu.VMEM)


def smem():
    return pl.BlockSpec(memory_space=pltpu.SMEM)


def hbm():
    return pl.BlockSpec(memory_space=pltpu.HBM)


def params(limit=20):
    return pltpu.CompilerParams(vmem_limit_bytes=limit << 20)


def as_row(tile):
    return jnp.sum(tile.T, axis=0, keepdims=True)


def lane_blocks(array, width=128):
    return [array[:, k : k + width] for k in range(0, array.shape[1], width)]


def in_parts(row):
    high = row.astype(BF16)
    rest = row - high.astype(F32)
    middle = rest.astype(BF16)
    low = (rest - middle.astype(F32)).astype(BF16)
    return high.astype(F32), middle.astype(F32), low.astype(F32)


def rows_of(parts, height, width):
    at = lax.broadcasted_iota(jnp.int32, (height, width), 0)
    out = jnp.zeros((height, width), F32)
    for k, part in enumerate(parts):
        out = jnp.where(at == k, part, out)
    return out


def before_kernel(
    slots, owners, per_owner, w_parts,
    index, count, probs_h, values_h, hidden_h, weight_h,
    outgoing, logits, stats,
    probs, values, hidden, weight, mapped, first, second, place, sems,
):
    blk = values.shape[-1]
    depth = weight.shape[0] // w_parts
    copies = [
        pltpu.make_async_copy(probs_h, probs, sems.at[0]),
        pltpu.make_async_copy(values_h, values, sems.at[1]),
        pltpu.make_async_copy(hidden_h, hidden, sems.at[2]),
    ] + [
        pltpu.make_async_copy(
            weight_h.at[pl.ds(k * depth, depth)], weight.at[pl.ds(k * depth, depth)], sems.at[3 + k]
        )
        for k in range(w_parts)
    ]
    for copy in copies:
        copy.start()
    for o in range(owners):
        first[o] = -1
        second[o] = -1
    live_slots = count[0]
    for s in range(slots):
        live = s < live_slots
        column = jnp.where(live, index[s, 1], 0)
        owner = column // per_owner
        had = first[owner]
        other = jnp.logical_and(had >= 0, had != column)
        first[owner] = jnp.where(jnp.logical_and(live, had < 0), column, had)
        second[owner] = jnp.where(jnp.logical_and(live, other), column, second[owner])
        place[s] = jnp.where(live, owner * CAP + jnp.where(other, 1, 0), owners * CAP)
    mapped[...] = jnp.zeros_like(mapped)
    copies[0].wait()
    copies[1].wait()
    for s in range(slots):
        row = jnp.where(s < live_slots, index[s, 0], 0)
        at = pl.multiple_of(row * blk, blk)
        block = jnp.dot(probs[:, pl.ds(at, blk)], values[s], preferred_element_type=F32)
        mapped[place[s]] += block
    mass = jnp.zeros((probs.shape[0], blk), F32)
    for o in range(owners):
        for c in range(CAP):
            piece = mapped[o * CAP + c].astype(BF16)
            outgoing[o, c * blk : (c + 1) * blk, :] = piece
            mass = mass + piece.astype(F32)
        label_a = lax.rem(jnp.maximum(first[o], 0), per_owner).astype(F32)
        label_b = lax.rem(jnp.maximum(second[o], 0), per_owner).astype(F32)
        at = lax.broadcasted_iota(jnp.int32, (EXTRA, blk), 0)
        outgoing[o, CAP * blk :, :] = jnp.where(at == 0, label_a, label_b).astype(BF16)
    copies[2].wait()
    total = jnp.zeros(logits.shape, F32)
    for k in range(w_parts):
        copies[3 + k].wait()
        total = total + jnp.dot(
            hidden[:, k * depth : (k + 1) * depth],
            weight[k * depth : (k + 1) * depth, :],
            preferred_element_type=F32,
        )
    logits[...] = total
    parts = lane_blocks(total)
    top = parts[0]
    for part in parts[1:]:
        top = jnp.maximum(top, part)
    largest = jnp.max(top, axis=1, keepdims=True)
    sums = sum(jnp.exp(part - largest) for part in parts)
    largest_row = jnp.max(top.T, axis=0, keepdims=True)
    lse = largest_row + jnp.log(as_row(sums))
    mass_row = as_row(mass)
    both = jnp.concatenate([lse, mass_row], axis=0)
    stats[...] = jnp.broadcast_to(both[None], stats.shape)


def between_kernel(stats, logits, soft, inverse, finals):
    lses = stats[:, 0, :]
    top = jnp.max(lses, axis=0, keepdims=True)
    lse = top + jnp.log(jnp.sum(jnp.exp(lses - top), axis=0, keepdims=True))
    mass = jnp.sum(stats[:, 1, :], axis=0, keepdims=True)
    tokens = lse.shape[1]
    lse_column = jnp.broadcast_to(lse, (tokens, tokens)).T
    inverse[...] = jnp.broadcast_to(LOSS_SCALE / mass, (tokens, tokens)).T
    for k in range(0, logits.shape[1], 128):
        soft[:, k : k + 128] = LOSS_SCALE * jnp.exp(logits[:, k : k + 128] - lse_column)
    finals[...] = jnp.concatenate([1.0 / mass, lse - jnp.log(mass)], axis=0)


def middle_kernel(per_owner, chunks, received, logits, soft, inverse, weight, grad, outgoing):
    sources = received.shape[0]
    blk = received.shape[2]
    scale = inverse[...]
    spread = jnp.zeros(scale.shape, F32)
    masses = [jnp.zeros(scale.shape, F32) for _ in range(per_owner)]
    for s in range(sources):
        labels = received[s, CAP * blk :, :].astype(F32)
        for c in range(CAP):
            label = labels[c : c + 1, :]
            piece = received[s, c * blk : (c + 1) * blk, :].astype(F32)
            for b in range(per_owner):
                masses[b] = masses[b] + jnp.where(label == float(b), piece, 0.0)
    for b in range(per_owner):
        at = slice(b * blk, (b + 1) * blk)
        mass = masses[b]
        positive = mass > 0
        spread = spread + jnp.where(
            positive, mass * (jnp.log(jnp.where(positive, mass, 1.0)) - logits[:, at]), 0.0
        )
        grad[:, at] = (soft[:, at] - mass * scale).astype(BF16)
    tail = rows_of(in_parts(as_row(spread)), EXTRA, blk).astype(BF16)
    owners, height = outgoing.shape[0], outgoing.shape[1] - EXTRA
    step = owners // chunks
    grads = grad[...]
    for k in range(chunks):
        rows = lax.dot_general(
            weight[k * step * height : (k + 1) * step * height, :], grads,
            (((1,), (1,)), ((), ())), preferred_element_type=F32,
        ).astype(BF16)
        for o in range(step):
            outgoing[k * step + o, :height, :] = rows[o * height : (o + 1) * height]
            outgoing[k * step + o, height:, :] = tail


def head_kernel(mine, other, grad_mine, grad_other, out):
    dims = (((0,), (0,)), ((), ()))
    out[...] = (
        lax.dot_general(mine[...], grad_mine[...], dims, preferred_element_type=F32)
        + lax.dot_general(other[...], grad_other[...], dims, preferred_element_type=F32)
    ).astype(BF16)


def half_sum_kernel(received, outgoing):
    total = received[0].astype(F32)
    for s in range(1, received.shape[0]):
        total = total + received[s].astype(F32)
    owners, height = outgoing.shape[0], outgoing.shape[1] - EXTRA
    spread = jnp.sum(total[owners * height : owners * height + 3], axis=0, keepdims=True)
    tail = rows_of(in_parts(spread), EXTRA, total.shape[1]).astype(BF16)
    for o in range(owners):
        outgoing[o, :height, :] = total[o * height : (o + 1) * height].astype(BF16)
        outgoing[o, height:, :] = tail


def last_sum_kernel(received, finals, divergence, grad_hidden):
    total = received[0].astype(F32)
    for s in range(1, received.shape[0]):
        total = total + received[s].astype(F32)
    height = grad_hidden.shape[0]
    grad_hidden[...] = total[:height]
    spread = jnp.sum(total[height : height + 3], axis=0, keepdims=True)
    divergence[...] = spread * finals[0:1, :] + finals[1:2, :]


def local(teacher_probs, block_values, block_index, block_count, hidden, student_weight):
    tokens, width = hidden.shape
    slots, blk = block_values.shape[2], block_values.shape[-1]
    owners, svocs = lax.axis_size(TVOC), lax.axis_size("svoc")
    everyone = owners * svocs
    shard = student_weight.shape[1]
    per_owner = shard // blk
    shape = jax.ShapeDtypeStruct
    w_parts = 6
    half = width // lax.axis_size("dp")
    me = lax.axis_index("dp")
    swap = [(0, 1), (1, 0)]
    hidden_mine = lax.dynamic_slice_in_dim(hidden, me * half, half, 1)
    hidden_other = lax.ppermute(
        lax.dynamic_slice_in_dim(hidden, (1 - me) * half, half, 1), "dp", swap
    )

    def before(*refs):
        before_kernel(slots, owners, per_owner, w_parts, *refs)

    outgoing, logits, stats = pl.pallas_call(
        before,
        out_shape=(
            shape((owners, CAP * blk + EXTRA, blk), BF16),
            shape((tokens, shard), F32),
            shape((everyone, 2, tokens), F32),
        ),
        in_specs=[smem(), smem(), hbm(), hbm(), hbm(), hbm()],
        out_specs=(vmem(), vmem(), vmem()),
        scratch_shapes=[
            pltpu.VMEM(teacher_probs.shape, BF16),
            pltpu.VMEM(block_values.shape[2:], BF16),
            pltpu.VMEM(hidden.shape, BF16),
            pltpu.VMEM(student_weight.shape, BF16),
            pltpu.VMEM((owners * CAP + 1, tokens, blk), F32),
            pltpu.SMEM((owners,), jnp.int32),
            pltpu.SMEM((owners,), jnp.int32),
            pltpu.SMEM((slots,), jnp.int32),
            pltpu.SemaphoreType.DMA((3 + w_parts,)),
        ],
        compiler_params=params(56),
        name="before",
    )(
        block_index[0, 0], block_count[0], teacher_probs, block_values[0, 0], hidden, student_weight
    )
    all_stats = lax.all_to_all(stats, TVOC_SVOC, 0, 0, tiled=True)
    received = lax.all_to_all(outgoing, TVOC, 0, 0, tiled=True)
    soft, inverse, finals = pl.pallas_call(
        between_kernel,
        out_shape=(
            shape((tokens, shard), F32), shape((tokens, tokens), F32), shape((2, tokens), F32),
        ),
        in_specs=[vmem()] * 2,
        out_specs=(vmem(),) * 3,
        compiler_params=params(),
        name="between",
    )(all_stats, logits)

    height = width // owners

    def middle(*refs):
        middle_kernel(per_owner, 4, *refs)

    grad, partial_hidden = pl.pallas_call(
        middle,
        out_shape=(shape((tokens, shard), BF16), shape((owners, height + EXTRA, tokens), BF16)),
        in_specs=[vmem()] * 5,
        out_specs=(vmem(),) * 2,
        compiler_params=params(),
        name="middle",
    )(received, logits, soft, inverse, student_weight)
    grad_other = lax.ppermute(grad, "dp", swap)
    summed = lax.all_to_all(partial_hidden, TVOC, 0, 0, tiled=True)
    tiles = 4
    grad_weight = pl.pallas_call(
        head_kernel,
        out_shape=shape((half, shard), BF16),
        grid=(tiles,),
        in_specs=[
            pl.BlockSpec((tokens, half // tiles), lambda i: (0, i)),
            pl.BlockSpec((tokens, half // tiles), lambda i: (0, i)),
            pl.BlockSpec((tokens, shard), lambda i: (0, 0)),
            pl.BlockSpec((tokens, shard), lambda i: (0, 0)),
        ],
        out_specs=pl.BlockSpec((half // tiles, shard), lambda i: (i, 0)),
        compiler_params=params(),
        name="head",
    )(hidden_mine, hidden_other, grad, grad_other)
    last = height // svocs
    nearer = pl.pallas_call(
        half_sum_kernel,
        out_shape=shape((svocs, last + EXTRA, tokens), BF16),
        in_specs=[vmem()],
        out_specs=vmem(),
        compiler_params=params(),
        name="half_sum",
    )(summed)
    arrived = lax.all_to_all(nearer, "svoc", 0, 0, tiled=True)
    divergence, grad_hidden = pl.pallas_call(
        last_sum_kernel,
        out_shape=(shape((1, tokens), F32), shape((last, tokens), F32)),
        in_specs=[vmem()] * 2,
        out_specs=(vmem(),) * 2,
        compiler_params=params(),
        name="last_sum",
    )(arrived, finals)
    return (divergence[0], grad_weight, grad_hidden.T)


def solution(mesh):
    finer = Mesh(
        mesh.devices.reshape(mesh.shape["dp"], 4, 4, mesh.shape["svoc"]),
        ("dp", "tvoc_0", "tvoc_1", "svoc"),
    )
    placed = (
        P("dp", TVOC),
        P(TVOC, "svoc", None, None, None),
        P(TVOC, "svoc", None, None),
        P(TVOC, "svoc"),
        P("dp", None),
        P(None, TVOC_SVOC),
    )
    return jax.shard_map(
        local,
        mesh=finer,
        in_specs=placed,
        out_specs=(P("dp"), P("dp", TVOC_SVOC), P("dp", TVOC_SVOC)),
        check_vma=False,
    )
```

```python
import jax
import jax.numpy as jnp
from jax import lax
from jax.experimental import pallas as pl
from jax.experimental.pallas import tpu as pltpu
from jax.sharding import Mesh
from jax.sharding import PartitionSpec as P

CAP = 2
TVOC = ("tvoc_0", "tvoc_1")
TVOC_SVOC = ("tvoc_0", "tvoc_1", "svoc")
LOSS_SCALE = 128.0
F32 = jnp.float32
BF16 = jnp.bfloat16
EXTRA = 8


def vmem():
    return pl.BlockSpec(memory_space=pltpu.VMEM)


def smem():
    return pl.BlockSpec(memory_space=pltpu.SMEM)


def hbm():
    return pl.BlockSpec(memory_space=pltpu.HBM)


def params(limit=20):
    return pltpu.CompilerParams(vmem_limit_bytes=limit << 20)


def as_row(tile):
    return jnp.sum(tile.T, axis=0, keepdims=True)


def lane_blocks(array, width=128):
    return [array[:, k : k + width] for k in range(0, array.shape[1], width)]


def in_parts(row):
    high = row.astype(BF16)
    rest = row - high.astype(F32)
    middle = rest.astype(BF16)
    low = (rest - middle.astype(F32)).astype(BF16)
    return high.astype(F32), middle.astype(F32), low.astype(F32)


def rows_of(parts, height, width):
    at = lax.broadcasted_iota(jnp.int32, (height, width), 0)
    out = jnp.zeros((height, width), F32)
    for k, part in enumerate(parts):
        out = jnp.where(at == k, part, out)
    return out


def before_kernel(
    slots, owners, per_owner, w_parts,
    index, count, probs_h, values_h, hidden_h, weight_h,
    outgoing, logits, stats, labels,
    probs, values, hidden, weight, mapped, first, second, place, sems,
):
    blk = values.shape[-1]
    depth = weight.shape[0] // w_parts
    copies = [
        pltpu.make_async_copy(probs_h, probs, sems.at[0]),
        pltpu.make_async_copy(values_h, values, sems.at[1]),
        pltpu.make_async_copy(hidden_h, hidden, sems.at[2]),
    ] + [
        pltpu.make_async_copy(
            weight_h.at[pl.ds(k * depth, depth)], weight.at[pl.ds(k * depth, depth)], sems.at[3 + k]
        )
        for k in range(w_parts)
    ]
    for copy in copies:
        copy.start()
    for o in range(owners):
        first[o] = -1
        second[o] = -1
    live_slots = count[0, 0]
    for s in range(slots):
        live = s < live_slots
        column = jnp.where(live, index[1, s], 0)
        owner = column // per_owner
        had = first[owner]
        other = jnp.logical_and(had >= 0, had != column)
        first[owner] = jnp.where(jnp.logical_and(live, had < 0), column, had)
        second[owner] = jnp.where(jnp.logical_and(live, other), column, second[owner])
        place[s] = jnp.where(live, owner * CAP + jnp.where(other, 1, 0), owners * CAP)
    mapped[...] = jnp.zeros_like(mapped)
    copies[0].wait()
    copies[1].wait()
    for s in range(slots):
        row = jnp.where(s < live_slots, index[0, s], 0)
        at = pl.multiple_of(row * blk, blk)
        block = jnp.dot(probs[:, pl.ds(at, blk)], values[s], preferred_element_type=F32)
        mapped[place[s]] += block
    mass = jnp.zeros((probs.shape[0], blk), F32)
    for o in range(owners):
        for c in range(CAP):
            piece = mapped[o * CAP + c].astype(BF16)
            outgoing[o, c * blk : (c + 1) * blk, :] = piece
            mass = mass + piece.astype(F32)
        label_a = lax.rem(jnp.maximum(first[o], 0), per_owner).astype(F32)
        label_b = lax.rem(jnp.maximum(second[o], 0), per_owner).astype(F32)
        at = lax.broadcasted_iota(jnp.int32, (EXTRA, blk), 0)
        labels[o] = jnp.where(at == 0, label_a, jnp.where(at == 1, label_b, 0.0))
    copies[2].wait()
    total = jnp.zeros(logits.shape, F32)
    for k in range(w_parts):
        copies[3 + k].wait()
        total = total + jnp.dot(
            hidden[:, k * depth : (k + 1) * depth],
            weight[k * depth : (k + 1) * depth, :],
            preferred_element_type=F32,
        )
    logits[...] = total
    parts = lane_blocks(total)
    top = parts[0]
    for part in parts[1:]:
        top = jnp.maximum(top, part)
    largest = jnp.max(top, axis=1, keepdims=True)
    sums = sum(jnp.exp(part - largest) for part in parts)
    largest_row = jnp.max(top.T, axis=0, keepdims=True)
    lse = largest_row + jnp.log(as_row(sums))
    mass_row = as_row(mass)
    both = jnp.concatenate([lse, mass_row], axis=0)
    stats[...] = jnp.broadcast_to(both[None], stats.shape)


def combined(lses, masses):
    top = jnp.max(lses, axis=0, keepdims=True)
    lse = top + jnp.log(jnp.sum(jnp.exp(lses - top), axis=0, keepdims=True))
    return lse, jnp.sum(masses, axis=0, keepdims=True)


def tail_kernel(stats, labels, _, outgoing, tails, sem):
    count = stats.shape[0]
    lse, mass = combined(
        jnp.concatenate([stats[k, 0:1, :] for k in range(count)], axis=0),
        jnp.concatenate([stats[k, 1:2, :] for k in range(count)], axis=0),
    )
    blk = lse.shape[1]
    added = rows_of([0.0, 0.0, *in_parts(lse), *in_parts(mass)], EXTRA, blk)
    for o in range(tails.shape[0]):
        tails[o] = (labels[o] + added).astype(BF16)
    copy = pltpu.make_async_copy(tails, outgoing.at[:, pl.ds(CAP * blk, EXTRA), :], sem)
    copy.start()
    copy.wait()


def middle_kernel(per_owner, chunks, received, logits, weight, grad, outgoing, finals):
    sources = received.shape[0]
    blk = received.shape[2]
    tails = [received[s, CAP * blk :, :].astype(F32) for s in range(sources)]
    lse, mass_sum = combined(
        jnp.concatenate([jnp.sum(t[2:5], axis=0, keepdims=True) for t in tails], axis=0),
        jnp.concatenate([jnp.sum(t[5:8], axis=0, keepdims=True) for t in tails], axis=0),
    )
    finals[...] = jnp.concatenate([1.0 / mass_sum, lse - jnp.log(mass_sum)], axis=0)
    lse_column = jnp.broadcast_to(lse, (blk, blk)).T
    scale = jnp.broadcast_to(LOSS_SCALE / mass_sum, (blk, blk)).T
    spread = jnp.zeros(scale.shape, F32)
    masses = [jnp.zeros(scale.shape, F32) for _ in range(per_owner)]
    for s in range(sources):
        for c in range(CAP):
            label = tails[s][c : c + 1, :]
            piece = received[s, c * blk : (c + 1) * blk, :].astype(F32)
            for b in range(per_owner):
                masses[b] = masses[b] + jnp.where(label == float(b), piece, 0.0)
    for b in range(per_owner):
        at = slice(b * blk, (b + 1) * blk)
        mass = masses[b]
        positive = mass > 0
        spread = spread + jnp.where(
            positive, mass * (jnp.log(jnp.where(positive, mass, 1.0)) - logits[:, at]), 0.0
        )
        soft = LOSS_SCALE * jnp.exp(logits[:, at] - lse_column)
        grad[:, at] = (soft - mass * scale).astype(BF16)
    tail = rows_of(in_parts(as_row(spread)), EXTRA, blk).astype(BF16)
    owners, height = outgoing.shape[0], outgoing.shape[1] - EXTRA
    step = owners // chunks
    grads = grad[...]
    for k in range(chunks):
        rows = lax.dot_general(
            weight[k * step * height : (k + 1) * step * height, :], grads,
            (((1,), (1,)), ((), ())), preferred_element_type=F32,
        ).astype(BF16)
        for o in range(step):
            outgoing[k * step + o, :height, :] = rows[o * height : (o + 1) * height]
            outgoing[k * step + o, height:, :] = tail


def head_kernel(mine, other, grad_mine, grad_other, out):
    dims = (((0,), (0,)), ((), ()))
    out[...] = (
        lax.dot_general(mine[...], grad_mine[...], dims, preferred_element_type=F32)
        + lax.dot_general(other[...], grad_other[...], dims, preferred_element_type=F32)
    ).astype(BF16)


def half_sum_kernel(received, outgoing):
    total = received[0].astype(F32)
    for s in range(1, received.shape[0]):
        total = total + received[s].astype(F32)
    owners, height = outgoing.shape[0], outgoing.shape[1] - EXTRA
    spread = jnp.sum(total[owners * height : owners * height + 3], axis=0, keepdims=True)
    tail = rows_of(in_parts(spread), EXTRA, total.shape[1]).astype(BF16)
    for o in range(owners):
        outgoing[o, :height, :] = total[o * height : (o + 1) * height].astype(BF16)
        outgoing[o, height:, :] = tail


def last_sum_kernel(received, finals, divergence, grad_hidden):
    total = received[0].astype(F32)
    for s in range(1, received.shape[0]):
        total = total + received[s].astype(F32)
    height = grad_hidden.shape[0]
    grad_hidden[...] = total[:height]
    spread = jnp.sum(total[height : height + 3], axis=0, keepdims=True)
    divergence[...] = spread * finals[0:1, :] + finals[1:2, :]


def local(teacher_probs, block_values, block_index, block_count, hidden, student_weight):
    tokens, width = hidden.shape
    slots, blk = block_values.shape[2], block_values.shape[-1]
    owners, svocs = lax.axis_size(TVOC), lax.axis_size("svoc")
    shard = student_weight.shape[1]
    per_owner = shard // blk
    shape = jax.ShapeDtypeStruct
    w_parts = 6
    half = width // lax.axis_size("dp")
    me = lax.axis_index("dp")
    swap = [(0, 1), (1, 0)]
    hidden_mine = lax.dynamic_slice_in_dim(hidden, me * half, half, 1)
    hidden_other = lax.ppermute(
        lax.dynamic_slice_in_dim(hidden, (1 - me) * half, half, 1), "dp", swap
    )

    def before(*refs):
        before_kernel(slots, owners, per_owner, w_parts, *refs)

    outgoing, logits, stats, labels = pl.pallas_call(
        before,
        out_shape=(
            shape((owners, CAP * blk + EXTRA, blk), BF16),
            shape((tokens, shard), F32),
            shape((svocs, 2, tokens), F32),
            shape((owners, EXTRA, blk), F32),
        ),
        in_specs=[smem(), smem(), hbm(), hbm(), hbm(), hbm()],
        out_specs=(vmem(),) * 4,
        scratch_shapes=[
            pltpu.VMEM(teacher_probs.shape, BF16),
            pltpu.VMEM(block_values.shape[2:], BF16),
            pltpu.VMEM(hidden.shape, BF16),
            pltpu.VMEM(student_weight.shape, BF16),
            pltpu.VMEM((owners * CAP + 1, tokens, blk), F32),
            pltpu.SMEM((owners,), jnp.int32),
            pltpu.SMEM((owners,), jnp.int32),
            pltpu.SMEM((slots,), jnp.int32),
            pltpu.SemaphoreType.DMA((3 + w_parts,)),
        ],
        compiler_params=params(56),
        name="before",
    )(
        block_index[0, 0].T, block_count, teacher_probs, block_values[0, 0], hidden, student_weight
    )
    near_stats = lax.all_to_all(stats, "svoc", 0, 0, tiled=True)
    outgoing = pl.pallas_call(
        tail_kernel,
        out_shape=shape(outgoing.shape, BF16),
        in_specs=[vmem(), vmem(), hbm()],
        out_specs=hbm(),
        scratch_shapes=[pltpu.VMEM((owners, EXTRA, blk), BF16), pltpu.SemaphoreType.DMA],
        input_output_aliases={2: 0},
        compiler_params=params(),
        name="tail",
    )(near_stats, labels, outgoing)
    received = lax.all_to_all(outgoing, TVOC, 0, 0, tiled=True)
    height = width // owners

    def middle(*refs):
        middle_kernel(per_owner, 4, *refs)

    grad, partial_hidden, finals = pl.pallas_call(
        middle,
        out_shape=(
            shape((tokens, shard), BF16),
            shape((owners, height + EXTRA, tokens), BF16),
            shape((2, tokens), F32),
        ),
        in_specs=[vmem()] * 3,
        out_specs=(vmem(),) * 3,
        compiler_params=params(),
        name="middle",
    )(received, logits, student_weight)
    grad_other = lax.ppermute(grad, "dp", swap)
    summed = lax.all_to_all(partial_hidden, TVOC, 0, 0, tiled=True)
    tiles = 4
    grad_weight = pl.pallas_call(
        head_kernel,
        out_shape=shape((half, shard), BF16),
        grid=(tiles,),
        in_specs=[
            pl.BlockSpec((tokens, half // tiles), lambda i: (0, i)),
            pl.BlockSpec((tokens, half // tiles), lambda i: (0, i)),
            pl.BlockSpec((tokens, shard), lambda i: (0, 0)),
            pl.BlockSpec((tokens, shard), lambda i: (0, 0)),
        ],
        out_specs=pl.BlockSpec((half // tiles, shard), lambda i: (i, 0)),
        compiler_params=params(),
        name="head",
    )(hidden_mine, hidden_other, grad, grad_other)
    last = height // svocs
    nearer = pl.pallas_call(
        half_sum_kernel,
        out_shape=shape((svocs, last + EXTRA, tokens), BF16),
        in_specs=[vmem()],
        out_specs=vmem(),
        compiler_params=params(),
        name="half_sum",
    )(summed)
    arrived = lax.all_to_all(nearer, "svoc", 0, 0, tiled=True)
    divergence, grad_hidden = pl.pallas_call(
        last_sum_kernel,
        out_shape=(shape((1, tokens), F32), shape((last, tokens), F32)),
        in_specs=[vmem()] * 2,
        out_specs=(vmem(),) * 2,
        compiler_params=params(),
        name="last_sum",
    )(arrived, finals)
    return (divergence[0], grad_weight, grad_hidden.T)


def solution(mesh):
    finer = Mesh(
        mesh.devices.reshape(mesh.shape["dp"], 4, 4, mesh.shape["svoc"]),
        ("dp", "tvoc_0", "tvoc_1", "svoc"),
    )
    placed = (
        P("dp", TVOC),
        P(TVOC, "svoc", None, None, None),
        P(TVOC, "svoc", None, None),
        P(TVOC, "svoc"),
        P("dp", None),
        P(None, TVOC_SVOC),
    )
    return jax.shard_map(
        local,
        mesh=finer,
        in_specs=placed,
        out_specs=(P("dp"), P("dp", TVOC_SVOC), P("dp", TVOC_SVOC)),
        check_vma=False,
    )
```

```python
import jax
import jax.numpy as jnp
from jax import lax
from jax.experimental import pallas as pl
from jax.experimental.pallas import tpu as pltpu
from jax.sharding import Mesh
from jax.sharding import PartitionSpec as P

CAP = 2
TVOC = ("tvoc_0", "tvoc_1")
TVOC_SVOC = ("tvoc_0", "tvoc_1", "svoc")
LOSS_SCALE = 128.0
F32 = jnp.float32
BF16 = jnp.bfloat16
EXTRA = 8


def vmem():
    return pl.BlockSpec(memory_space=pltpu.VMEM)


def smem():
    return pl.BlockSpec(memory_space=pltpu.SMEM)


def hbm():
    return pl.BlockSpec(memory_space=pltpu.HBM)


def params(limit=20):
    return pltpu.CompilerParams(vmem_limit_bytes=limit << 20)


def as_row(tile):
    return jnp.sum(tile.T, axis=0, keepdims=True)


def lane_blocks(array, width=128):
    return [array[:, k : k + width] for k in range(0, array.shape[1], width)]


def in_parts(row):
    high = row.astype(BF16)
    rest = row - high.astype(F32)
    middle = rest.astype(BF16)
    low = (rest - middle.astype(F32)).astype(BF16)
    return high.astype(F32), middle.astype(F32), low.astype(F32)


def rows_of(parts, height, width):
    at = lax.broadcasted_iota(jnp.int32, (height, width), 0)
    out = jnp.zeros((height, width), F32)
    for k, part in enumerate(parts):
        out = jnp.where(at == k, part, out)
    return out


def stats_kernel(
    slots, w_parts,
    index, count, probs_h, values_h, hidden_h, weight_h,
    logits, stats,
    probs, values, hidden, weight, sems,
):
    blk = values.shape[-1]
    depth = weight.shape[0] // w_parts
    copies = [
        pltpu.make_async_copy(values_h, values, sems.at[0]),
        pltpu.make_async_copy(probs_h, probs, sems.at[1]),
        pltpu.make_async_copy(hidden_h, hidden, sems.at[2]),
    ] + [
        pltpu.make_async_copy(
            weight_h.at[pl.ds(k * depth, depth)], weight.at[pl.ds(k * depth, depth)], sems.at[3 + k]
        )
        for k in range(w_parts)
    ]
    for copy in copies:
        copy.start()
    live_slots = count[0, 0]
    copies[0].wait()
    copies[1].wait()
    mass = jnp.zeros((probs.shape[0], blk), F32)
    for s in range(slots):
        live = s < live_slots
        at = pl.multiple_of(jnp.where(live, index[0, s], 0) * blk, blk)
        block = jnp.dot(probs[:, pl.ds(at, blk)], values[s], preferred_element_type=F32)
        mass = mass + jnp.where(live, block, 0.0)
    mass_row = as_row(mass)
    copies[2].wait()
    total = jnp.zeros(logits.shape, F32)
    for k in range(w_parts):
        copies[3 + k].wait()
        total = total + jnp.dot(
            hidden[:, k * depth : (k + 1) * depth],
            weight[k * depth : (k + 1) * depth, :],
            preferred_element_type=F32,
        )
    logits[...] = total
    parts = lane_blocks(total)
    top = parts[0]
    for part in parts[1:]:
        top = jnp.maximum(top, part)
    largest = jnp.max(top, axis=1, keepdims=True)
    sums = sum(jnp.exp(part - largest) for part in parts)
    largest_row = jnp.max(top.T, axis=0, keepdims=True)
    lse = largest_row + jnp.log(as_row(sums))
    both = jnp.concatenate([lse, mass_row], axis=0)
    stats[...] = jnp.broadcast_to(both[None], stats.shape)


def mapping_kernel(
    slots, owners, per_owner,
    index, count, probs_h, values_h,
    outgoing,
    probs, values, mapped, first, second, place, sems,
):
    blk = values.shape[-1]
    copies = [
        pltpu.make_async_copy(values_h, values, sems.at[0]),
        pltpu.make_async_copy(probs_h, probs, sems.at[1]),
    ]
    for copy in copies:
        copy.start()
    for o in range(owners):
        first[o] = -1
        second[o] = -1
    live_slots = count[0, 0]
    for s in range(slots):
        live = s < live_slots
        column = jnp.where(live, index[1, s], 0)
        owner = column // per_owner
        had = first[owner]
        other = jnp.logical_and(had >= 0, had != column)
        first[owner] = jnp.where(jnp.logical_and(live, had < 0), column, had)
        second[owner] = jnp.where(jnp.logical_and(live, other), column, second[owner])
        place[s] = jnp.where(live, owner * CAP + jnp.where(other, 1, 0), owners * CAP)
    mapped[...] = jnp.zeros_like(mapped)
    for copy in copies:
        copy.wait()
    for s in range(slots):
        row = jnp.where(s < live_slots, index[0, s], 0)
        at = pl.multiple_of(row * blk, blk)
        block = jnp.dot(probs[:, pl.ds(at, blk)], values[s], preferred_element_type=F32)
        mapped[place[s]] += block
    for o in range(owners):
        for c in range(CAP):
            outgoing[o, c * blk : (c + 1) * blk, :] = mapped[o * CAP + c].astype(BF16)
        label_a = lax.rem(jnp.maximum(first[o], 0), per_owner).astype(F32)
        label_b = lax.rem(jnp.maximum(second[o], 0), per_owner).astype(F32)
        at = lax.broadcasted_iota(jnp.int32, (EXTRA, blk), 0)
        outgoing[o, CAP * blk :, :] = jnp.where(
            at == 0, label_a, jnp.where(at == 1, label_b, 0.0)
        ).astype(BF16)


def combined(lses, masses):
    top = jnp.max(lses, axis=0, keepdims=True)
    lse = top + jnp.log(jnp.sum(jnp.exp(lses - top), axis=0, keepdims=True))
    return lse, jnp.sum(masses, axis=0, keepdims=True)


def tail_kernel(stats, _, outgoing, tails, sems):
    there = outgoing.at[:, pl.ds(CAP * tails.shape[2], EXTRA), :]
    labels = pltpu.make_async_copy(there, tails, sems.at[0])
    labels.start()
    count = stats.shape[0]
    lse, mass = combined(
        jnp.concatenate([stats[k, 0:1, :] for k in range(count)], axis=0),
        jnp.concatenate([stats[k, 1:2, :] for k in range(count)], axis=0),
    )
    added = rows_of([0.0, 0.0, *in_parts(lse), *in_parts(mass)], EXTRA, lse.shape[1])
    labels.wait()
    for o in range(tails.shape[0]):
        tails[o] = (tails[o].astype(F32) + added).astype(BF16)
    copy = pltpu.make_async_copy(tails, there, sems.at[1])
    copy.start()
    copy.wait()


def middle_kernel(per_owner, chunks, received, logits, weight, grad, outgoing, finals):
    sources = received.shape[0]
    blk = received.shape[2]
    tails = [received[s, CAP * blk :, :].astype(F32) for s in range(sources)]
    lse, mass_sum = combined(
        jnp.concatenate([jnp.sum(t[2:5], axis=0, keepdims=True) for t in tails], axis=0),
        jnp.concatenate([jnp.sum(t[5:8], axis=0, keepdims=True) for t in tails], axis=0),
    )
    finals[...] = lse
    lse_column = jnp.broadcast_to(lse, (blk, blk)).T
    scale = jnp.broadcast_to(LOSS_SCALE / mass_sum, (blk, blk)).T
    spread = jnp.zeros(scale.shape, F32)
    masses = [jnp.zeros(scale.shape, F32) for _ in range(per_owner)]
    for s in range(sources):
        for c in range(CAP):
            label = tails[s][c : c + 1, :]
            piece = received[s, c * blk : (c + 1) * blk, :].astype(F32)
            for b in range(per_owner):
                masses[b] = masses[b] + jnp.where(label == float(b), piece, 0.0)
    for b in range(per_owner):
        at = slice(b * blk, (b + 1) * blk)
        mass = masses[b]
        positive = mass > 0
        spread = spread + jnp.where(
            positive, mass * (jnp.log(jnp.where(positive, mass, 1.0)) - logits[:, at]), 0.0
        )
        soft = LOSS_SCALE * jnp.exp(logits[:, at] - lse_column)
        grad[:, at] = (soft - mass * scale).astype(BF16)
    sums = [*in_parts(as_row(spread)), *in_parts(as_row(sum(masses[1:], masses[0])))]
    tail = rows_of(sums, EXTRA, blk).astype(BF16)
    owners, height = outgoing.shape[0], outgoing.shape[1] - EXTRA
    step = owners // chunks
    grads = grad[...]
    for k in range(chunks):
        rows = lax.dot_general(
            weight[k * step * height : (k + 1) * step * height, :], grads,
            (((1,), (1,)), ((), ())), preferred_element_type=F32,
        ).astype(BF16)
        for o in range(step):
            outgoing[k * step + o, :height, :] = rows[o * height : (o + 1) * height]
            outgoing[k * step + o, height:, :] = tail


def head_kernel(mine, other, grad_mine, grad_other, out):
    dims = (((0,), (0,)), ((), ()))
    out[...] = (
        lax.dot_general(mine[...], grad_mine[...], dims, preferred_element_type=F32)
        + lax.dot_general(other[...], grad_other[...], dims, preferred_element_type=F32)
    ).astype(BF16)


def half_sum_kernel(received, outgoing):
    total = received[0].astype(F32)
    for s in range(1, received.shape[0]):
        total = total + received[s].astype(F32)
    owners, height = outgoing.shape[0], outgoing.shape[1] - EXTRA
    sums = [
        part
        for at in (owners * height, owners * height + 3)
        for part in in_parts(jnp.sum(total[at : at + 3], axis=0, keepdims=True))
    ]
    tail = rows_of(sums, EXTRA, total.shape[1]).astype(BF16)
    for o in range(owners):
        outgoing[o, :height, :] = total[o * height : (o + 1) * height].astype(BF16)
        outgoing[o, height:, :] = tail


def last_sum_kernel(received, finals, divergence, grad_hidden):
    total = received[0].astype(F32)
    for s in range(1, received.shape[0]):
        total = total + received[s].astype(F32)
    height = grad_hidden.shape[0]
    grad_hidden[...] = total[:height]
    spread = jnp.sum(total[height : height + 3], axis=0, keepdims=True)
    mass = jnp.sum(total[height + 3 : height + 6], axis=0, keepdims=True)
    divergence[...] = spread / mass - jnp.log(mass) + finals[...]


def local(teacher_probs, block_values, block_index, block_count, hidden, student_weight):
    tokens, width = hidden.shape
    slots, blk = block_values.shape[2], block_values.shape[-1]
    owners, svocs = lax.axis_size(TVOC), lax.axis_size("svoc")
    shard = student_weight.shape[1]
    per_owner = shard // blk
    shape = jax.ShapeDtypeStruct
    w_parts = 6
    half = width // lax.axis_size("dp")
    me = lax.axis_index("dp")
    swap = [(0, 1), (1, 0)]
    hidden_mine = lax.dynamic_slice_in_dim(hidden, me * half, half, 1)
    hidden_other = lax.ppermute(
        lax.dynamic_slice_in_dim(hidden, (1 - me) * half, half, 1), "dp", swap
    )

    index, values = block_index[0, 0].T, block_values[0, 0]

    def stats_of(*refs):
        stats_kernel(slots, w_parts, *refs)

    logits, stats = pl.pallas_call(
        stats_of,
        out_shape=(shape((tokens, shard), F32), shape((svocs, 2, tokens), F32)),
        in_specs=[smem(), smem(), hbm(), hbm(), hbm(), hbm()],
        out_specs=(vmem(),) * 2,
        scratch_shapes=[
            pltpu.VMEM(teacher_probs.shape, BF16),
            pltpu.VMEM(values.shape, BF16),
            pltpu.VMEM(hidden.shape, BF16),
            pltpu.VMEM(student_weight.shape, BF16),
            pltpu.SemaphoreType.DMA((3 + w_parts,)),
        ],
        compiler_params=params(56),
        name="stats",
    )(index, block_count, teacher_probs, values, hidden, student_weight)
    near_stats = lax.all_to_all(stats, "svoc", 0, 0, tiled=True)

    def mapping(*refs):
        mapping_kernel(slots, owners, per_owner, *refs)

    outgoing = pl.pallas_call(
        mapping,
        out_shape=shape((owners, CAP * blk + EXTRA, blk), BF16),
        in_specs=[smem(), smem(), hbm(), hbm()],
        out_specs=vmem(),
        scratch_shapes=[
            pltpu.VMEM(teacher_probs.shape, BF16),
            pltpu.VMEM(values.shape, BF16),
            pltpu.VMEM((owners * CAP + 1, tokens, blk), F32),
            pltpu.SMEM((owners,), jnp.int32),
            pltpu.SMEM((owners,), jnp.int32),
            pltpu.SMEM((slots,), jnp.int32),
            pltpu.SemaphoreType.DMA((2,)),
        ],
        compiler_params=params(),
        cost_estimate=pl.CostEstimate(
            flops=2 * slots * tokens * blk * blk, bytes_accessed=4 << 20, transcendentals=0
        ),
        name="mapping",
    )(index, block_count, teacher_probs, values)
    outgoing = pl.pallas_call(
        tail_kernel,
        out_shape=shape(outgoing.shape, BF16),
        in_specs=[vmem(), hbm()],
        out_specs=hbm(),
        scratch_shapes=[pltpu.VMEM((owners, EXTRA, blk), BF16), pltpu.SemaphoreType.DMA((2,))],
        input_output_aliases={1: 0},
        compiler_params=params(),
        name="tail",
    )(near_stats, outgoing)
    received = lax.all_to_all(outgoing, TVOC, 0, 0, tiled=True)
    height = width // owners

    def middle(*refs):
        middle_kernel(per_owner, 4, *refs)

    grad, partial_hidden, finals = pl.pallas_call(
        middle,
        out_shape=(
            shape((tokens, shard), BF16),
            shape((owners, height + EXTRA, tokens), BF16),
            shape((1, tokens), F32),
        ),
        in_specs=[vmem()] * 3,
        out_specs=(vmem(),) * 3,
        compiler_params=params(),
        name="middle",
    )(received, logits, student_weight)
    grad_other = lax.ppermute(grad, "dp", swap)
    summed = lax.all_to_all(partial_hidden, TVOC, 0, 0, tiled=True)
    tiles = 4
    grad_weight = pl.pallas_call(
        head_kernel,
        out_shape=shape((half, shard), BF16),
        grid=(tiles,),
        in_specs=[
            pl.BlockSpec((tokens, half // tiles), lambda i: (0, i)),
            pl.BlockSpec((tokens, half // tiles), lambda i: (0, i)),
            pl.BlockSpec((tokens, shard), lambda i: (0, 0)),
            pl.BlockSpec((tokens, shard), lambda i: (0, 0)),
        ],
        out_specs=pl.BlockSpec((half // tiles, shard), lambda i: (i, 0)),
        compiler_params=params(),
        name="head",
    )(hidden_mine, hidden_other, grad, grad_other)
    last = height // svocs
    nearer = pl.pallas_call(
        half_sum_kernel,
        out_shape=shape((svocs, last + EXTRA, tokens), BF16),
        in_specs=[vmem()],
        out_specs=vmem(),
        compiler_params=params(),
        name="half_sum",
    )(summed)
    arrived = lax.all_to_all(nearer, "svoc", 0, 0, tiled=True)
    divergence, grad_hidden = pl.pallas_call(
        last_sum_kernel,
        out_shape=(shape((1, tokens), F32), shape((last, tokens), F32)),
        in_specs=[vmem()] * 2,
        out_specs=(vmem(),) * 2,
        compiler_params=params(),
        name="last_sum",
    )(arrived, finals)
    return (divergence[0], grad_weight, grad_hidden.T)


def solution(mesh):
    finer = Mesh(
        mesh.devices.reshape(mesh.shape["dp"], 4, 4, mesh.shape["svoc"]),
        ("dp", "tvoc_0", "tvoc_1", "svoc"),
    )
    placed = (
        P("dp", TVOC),
        P(TVOC, "svoc", None, None, None),
        P(TVOC, "svoc", None, None),
        P(TVOC, "svoc"),
        P("dp", None),
        P(None, TVOC_SVOC),
    )
    return jax.shard_map(
        local,
        mesh=finer,
        in_specs=placed,
        out_specs=(P("dp"), P("dp", TVOC_SVOC), P("dp", TVOC_SVOC)),
        check_vma=False,
    )
```

```python
import jax
import jax.numpy as jnp
from jax import lax
from jax.experimental import pallas as pl
from jax.experimental.pallas import tpu as pltpu
from jax.sharding import Mesh
from jax.sharding import PartitionSpec as P

CAP = 2
TVOC = ("tvoc_0", "tvoc_1")
TVOC_SVOC = ("tvoc_0", "tvoc_1", "svoc")
LOSS_SCALE = 128.0
F32 = jnp.float32
BF16 = jnp.bfloat16
EXTRA = 8


def vmem():
    return pl.BlockSpec(memory_space=pltpu.VMEM)


def hbm():
    return pl.BlockSpec(memory_space=pltpu.HBM)


def params(limit=20):
    return pltpu.CompilerParams(vmem_limit_bytes=limit << 20)


def as_row(tile):
    return jnp.sum(tile.T, axis=0, keepdims=True)


def lane_blocks(array, width=128):
    return [array[:, k : k + width] for k in range(0, array.shape[1], width)]


def in_parts(row):
    high = row.astype(BF16)
    rest = row - high.astype(F32)
    middle = rest.astype(BF16)
    low = (rest - middle.astype(F32)).astype(BF16)
    return high.astype(F32), middle.astype(F32), low.astype(F32)


def rows_of(parts, height, width):
    at = lax.broadcasted_iota(jnp.int32, (height, width), 0)
    out = jnp.zeros((height, width), F32)
    for k, part in enumerate(parts):
        out = jnp.where(at == k, part, out)
    return out


def stats_kernel(
    slots, w_parts,
    index_h, count_h, probs_h, values_h, hidden_h, weight_h,
    logits_h, stats,
    index, count, probs, values, hidden, weight, logits, sems,
):
    blk = values.shape[-1]
    depth = weight.shape[0] // w_parts
    small = [
        pltpu.make_async_copy(index_h, index, sems.at[3 + w_parts]),
        pltpu.make_async_copy(count_h, count, sems.at[4 + w_parts]),
    ]
    copies = [
        pltpu.make_async_copy(values_h, values, sems.at[0]),
        pltpu.make_async_copy(probs_h, probs, sems.at[1]),
        pltpu.make_async_copy(hidden_h, hidden, sems.at[2]),
    ] + [
        pltpu.make_async_copy(
            weight_h.at[pl.ds(k * depth, depth)], weight.at[pl.ds(k * depth, depth)], sems.at[3 + k]
        )
        for k in range(w_parts)
    ]
    for copy in small + copies:
        copy.start()
    for copy in small:
        copy.wait()
    live_slots = count[0, 0]
    copies[0].wait()
    copies[1].wait()
    mass = jnp.zeros((probs.shape[0], blk), F32)
    for s in range(slots):
        live = s < live_slots
        at = pl.multiple_of(jnp.where(live, index[0, s], 0) * blk, blk)
        block = jnp.dot(probs[:, pl.ds(at, blk)], values[s], preferred_element_type=F32)
        mass = mass + jnp.where(live, block, 0.0)
    mass_row = as_row(mass)
    copies[2].wait()
    total = jnp.zeros(logits.shape, F32)
    for k in range(w_parts):
        copies[3 + k].wait()
        total = total + jnp.dot(
            hidden[:, k * depth : (k + 1) * depth],
            weight[k * depth : (k + 1) * depth, :],
            preferred_element_type=F32,
        )
    logits[...] = total
    leaving = pltpu.make_async_copy(logits, logits_h, sems.at[5 + w_parts])
    leaving.start()
    parts = lane_blocks(total)
    top = parts[0]
    for part in parts[1:]:
        top = jnp.maximum(top, part)
    largest = jnp.max(top, axis=1, keepdims=True)
    sums = sum(jnp.exp(part - largest) for part in parts)
    largest_row = jnp.max(top.T, axis=0, keepdims=True)
    lse = largest_row + jnp.log(as_row(sums))
    both = jnp.concatenate([lse, mass_row], axis=0)
    stats[...] = jnp.broadcast_to(both[None], stats.shape)
    leaving.wait()


def mapping_kernel(
    slots, owners, per_owner,
    index_h, count_h, probs_h, values_h,
    outgoing,
    index, count, probs, values, mapped, first, second, place, sems,
):
    blk = values.shape[-1]
    small = [
        pltpu.make_async_copy(index_h, index, sems.at[2]),
        pltpu.make_async_copy(count_h, count, sems.at[3]),
    ]
    copies = [
        pltpu.make_async_copy(values_h, values, sems.at[0]),
        pltpu.make_async_copy(probs_h, probs, sems.at[1]),
    ]
    for copy in small + copies:
        copy.start()
    for o in range(owners):
        first[o] = -1
        second[o] = -1
    for copy in small:
        copy.wait()
    live_slots = count[0, 0]
    for s in range(slots):
        live = s < live_slots
        column = jnp.where(live, index[1, s], 0)
        owner = column // per_owner
        had = first[owner]
        other = jnp.logical_and(had >= 0, had != column)
        first[owner] = jnp.where(jnp.logical_and(live, had < 0), column, had)
        second[owner] = jnp.where(jnp.logical_and(live, other), column, second[owner])
        place[s] = jnp.where(live, owner * CAP + jnp.where(other, 1, 0), owners * CAP)
    mapped[...] = jnp.zeros_like(mapped)
    for copy in copies:
        copy.wait()
    for s in range(slots):
        row = jnp.where(s < live_slots, index[0, s], 0)
        at = pl.multiple_of(row * blk, blk)
        block = jnp.dot(probs[:, pl.ds(at, blk)], values[s], preferred_element_type=F32)
        mapped[place[s]] += block
    for o in range(owners):
        for c in range(CAP):
            outgoing[o, c * blk : (c + 1) * blk, :] = mapped[o * CAP + c].astype(BF16)
        label_a = lax.rem(jnp.maximum(first[o], 0), per_owner).astype(F32)
        label_b = lax.rem(jnp.maximum(second[o], 0), per_owner).astype(F32)
        at = lax.broadcasted_iota(jnp.int32, (EXTRA, blk), 0)
        outgoing[o, CAP * blk :, :] = jnp.where(
            at == 0, label_a, jnp.where(at == 1, label_b, 0.0)
        ).astype(BF16)


def combined(lses, masses):
    top = jnp.max(lses, axis=0, keepdims=True)
    lse = top + jnp.log(jnp.sum(jnp.exp(lses - top), axis=0, keepdims=True))
    return lse, jnp.sum(masses, axis=0, keepdims=True)


def tail_kernel(stats, _, outgoing, tails, sems):
    there = outgoing.at[:, pl.ds(CAP * tails.shape[2], EXTRA), :]
    labels = pltpu.make_async_copy(there, tails, sems.at[0])
    labels.start()
    count = stats.shape[0]
    lse, mass = combined(
        jnp.concatenate([stats[k, 0:1, :] for k in range(count)], axis=0),
        jnp.concatenate([stats[k, 1:2, :] for k in range(count)], axis=0),
    )
    added = rows_of([0.0, 0.0, *in_parts(lse), *in_parts(mass)], EXTRA, lse.shape[1])
    labels.wait()
    for o in range(tails.shape[0]):
        tails[o] = (tails[o].astype(F32) + added).astype(BF16)
    copy = pltpu.make_async_copy(tails, there, sems.at[1])
    copy.start()
    copy.wait()


def middle_kernel(per_owner, chunks, received, logits, weight, grad, outgoing, finals):
    sources = received.shape[0]
    blk = received.shape[2]
    tails = [received[s, CAP * blk :, :].astype(F32) for s in range(sources)]
    lse, mass_sum = combined(
        jnp.concatenate([jnp.sum(t[2:5], axis=0, keepdims=True) for t in tails], axis=0),
        jnp.concatenate([jnp.sum(t[5:8], axis=0, keepdims=True) for t in tails], axis=0),
    )
    finals[...] = lse
    lse_column = jnp.broadcast_to(lse, (blk, blk)).T
    scale = jnp.broadcast_to(LOSS_SCALE / mass_sum, (blk, blk)).T
    spread = jnp.zeros(scale.shape, F32)
    masses = [jnp.zeros(scale.shape, F32) for _ in range(per_owner)]
    for s in range(sources):
        for c in range(CAP):
            label = tails[s][c : c + 1, :]
            piece = received[s, c * blk : (c + 1) * blk, :].astype(F32)
            for b in range(per_owner):
                masses[b] = masses[b] + jnp.where(label == float(b), piece, 0.0)
    for b in range(per_owner):
        at = slice(b * blk, (b + 1) * blk)
        mass = masses[b]
        positive = mass > 0
        spread = spread + jnp.where(
            positive, mass * (jnp.log(jnp.where(positive, mass, 1.0)) - logits[:, at]), 0.0
        )
        soft = LOSS_SCALE * jnp.exp(logits[:, at] - lse_column)
        grad[:, at] = (soft - mass * scale).astype(BF16)
    sums = [*in_parts(as_row(spread)), *in_parts(as_row(sum(masses[1:], masses[0])))]
    tail = rows_of(sums, EXTRA, blk).astype(BF16)
    owners, height = outgoing.shape[0], outgoing.shape[1] - EXTRA
    step = owners // chunks
    grads = grad[...]
    for k in range(chunks):
        rows = lax.dot_general(
            weight[k * step * height : (k + 1) * step * height, :], grads,
            (((1,), (1,)), ((), ())), preferred_element_type=F32,
        ).astype(BF16)
        for o in range(step):
            outgoing[k * step + o, :height, :] = rows[o * height : (o + 1) * height]
            outgoing[k * step + o, height:, :] = tail


def head_kernel(mine, other, grad_mine, grad_other, out):
    dims = (((0,), (0,)), ((), ()))
    out[...] = (
        lax.dot_general(mine[...], grad_mine[...], dims, preferred_element_type=F32)
        + lax.dot_general(other[...], grad_other[...], dims, preferred_element_type=F32)
    ).astype(BF16)


def half_sum_kernel(received, outgoing):
    total = received[0].astype(F32)
    for s in range(1, received.shape[0]):
        total = total + received[s].astype(F32)
    owners, height = outgoing.shape[0], outgoing.shape[1] - EXTRA
    sums = [
        part
        for at in (owners * height, owners * height + 3)
        for part in in_parts(jnp.sum(total[at : at + 3], axis=0, keepdims=True))
    ]
    tail = rows_of(sums, EXTRA, total.shape[1]).astype(BF16)
    for o in range(owners):
        outgoing[o, :height, :] = total[o * height : (o + 1) * height].astype(BF16)
        outgoing[o, height:, :] = tail


def last_sum_kernel(received, finals, divergence, grad_hidden):
    total = received[0].astype(F32)
    for s in range(1, received.shape[0]):
        total = total + received[s].astype(F32)
    height = grad_hidden.shape[0]
    grad_hidden[...] = total[:height]
    spread = jnp.sum(total[height : height + 3], axis=0, keepdims=True)
    mass = jnp.sum(total[height + 3 : height + 6], axis=0, keepdims=True)
    divergence[...] = spread / mass - jnp.log(mass) + finals[...]


def local(teacher_probs, block_values, block_index, block_count, hidden, student_weight):
    tokens, width = hidden.shape
    slots, blk = block_values.shape[2], block_values.shape[-1]
    owners, svocs = lax.axis_size(TVOC), lax.axis_size("svoc")
    shard = student_weight.shape[1]
    per_owner = shard // blk
    shape = jax.ShapeDtypeStruct
    w_parts = 6
    half = width // lax.axis_size("dp")
    me = lax.axis_index("dp")
    swap = [(0, 1), (1, 0)]
    hidden_mine = lax.dynamic_slice_in_dim(hidden, me * half, half, 1)
    hidden_other = lax.ppermute(
        lax.dynamic_slice_in_dim(hidden, (1 - me) * half, half, 1), "dp", swap
    )

    index, values = block_index[0, 0].T, block_values[0, 0]

    def stats_of(*refs):
        stats_kernel(slots, w_parts, *refs)

    logits, stats = pl.pallas_call(
        stats_of,
        out_shape=(shape((tokens, shard), F32), shape((svocs, 2, tokens), F32)),
        in_specs=[hbm()] * 6,
        out_specs=(hbm(), vmem()),
        scratch_shapes=[
            pltpu.SMEM(index.shape, jnp.int32),
            pltpu.SMEM(block_count.shape, jnp.int32),
            pltpu.VMEM(teacher_probs.shape, BF16),
            pltpu.VMEM(values.shape, BF16),
            pltpu.VMEM(hidden.shape, BF16),
            pltpu.VMEM(student_weight.shape, BF16),
            pltpu.VMEM((tokens, shard), F32),
            pltpu.SemaphoreType.DMA((6 + w_parts,)),
        ],
        compiler_params=params(60),
        name="stats",
    )(index, block_count, teacher_probs, values, hidden, student_weight)
    near_stats = lax.all_to_all(stats, "svoc", 0, 0, tiled=True)

    def mapping(*refs):
        mapping_kernel(slots, owners, per_owner, *refs)

    outgoing = pl.pallas_call(
        mapping,
        out_shape=shape((owners, CAP * blk + EXTRA, blk), BF16),
        in_specs=[hbm()] * 4,
        out_specs=vmem(),
        scratch_shapes=[
            pltpu.SMEM(index.shape, jnp.int32),
            pltpu.SMEM(block_count.shape, jnp.int32),
            pltpu.VMEM(teacher_probs.shape, BF16),
            pltpu.VMEM(values.shape, BF16),
            pltpu.VMEM((owners * CAP + 1, tokens, blk), F32),
            pltpu.SMEM((owners,), jnp.int32),
            pltpu.SMEM((owners,), jnp.int32),
            pltpu.SMEM((slots,), jnp.int32),
            pltpu.SemaphoreType.DMA((4,)),
        ],
        compiler_params=params(),
        cost_estimate=pl.CostEstimate(
            flops=2 * slots * tokens * blk * blk, bytes_accessed=4 << 20, transcendentals=0
        ),
        name="mapping",
    )(index, block_count, teacher_probs, values)
    outgoing = pl.pallas_call(
        tail_kernel,
        out_shape=shape(outgoing.shape, BF16),
        in_specs=[vmem(), hbm()],
        out_specs=hbm(),
        scratch_shapes=[pltpu.VMEM((owners, EXTRA, blk), BF16), pltpu.SemaphoreType.DMA((2,))],
        input_output_aliases={1: 0},
        compiler_params=params(),
        name="tail",
    )(near_stats, outgoing)
    received = lax.all_to_all(outgoing, TVOC, 0, 0, tiled=True)
    height = width // owners

    def middle(*refs):
        middle_kernel(per_owner, 4, *refs)

    grad, partial_hidden, finals = pl.pallas_call(
        middle,
        out_shape=(
            shape((tokens, shard), BF16),
            shape((owners, height + EXTRA, tokens), BF16),
            shape((1, tokens), F32),
        ),
        in_specs=[vmem()] * 3,
        out_specs=(vmem(),) * 3,
        compiler_params=params(),
        name="middle",
    )(received, logits, student_weight)
    grad_other = lax.ppermute(grad, "dp", swap)
    summed = lax.all_to_all(partial_hidden, TVOC, 0, 0, tiled=True)
    tiles = 4
    grad_weight = pl.pallas_call(
        head_kernel,
        out_shape=shape((half, shard), BF16),
        grid=(tiles,),
        in_specs=[
            pl.BlockSpec((tokens, half // tiles), lambda i: (0, i)),
            pl.BlockSpec((tokens, half // tiles), lambda i: (0, i)),
            pl.BlockSpec((tokens, shard), lambda i: (0, 0)),
            pl.BlockSpec((tokens, shard), lambda i: (0, 0)),
        ],
        out_specs=pl.BlockSpec((half // tiles, shard), lambda i: (i, 0)),
        compiler_params=params(),
        name="head",
    )(hidden_mine, hidden_other, grad, grad_other)
    last = height // svocs
    summed, grad_weight = lax.optimization_barrier((summed, grad_weight))
    nearer = pl.pallas_call(
        half_sum_kernel,
        out_shape=shape((svocs, last + EXTRA, tokens), BF16),
        in_specs=[vmem()],
        out_specs=vmem(),
        compiler_params=params(),
        name="half_sum",
    )(summed)
    arrived = lax.all_to_all(nearer, "svoc", 0, 0, tiled=True)
    divergence, grad_hidden = pl.pallas_call(
        last_sum_kernel,
        out_shape=(shape((1, tokens), F32), shape((last, tokens), F32)),
        in_specs=[vmem()] * 2,
        out_specs=(vmem(),) * 2,
        compiler_params=params(),
        name="last_sum",
    )(arrived, finals)
    return (divergence[0], grad_weight, grad_hidden.T)


def solution(mesh):
    finer = Mesh(
        mesh.devices.reshape(mesh.shape["dp"], 4, 4, mesh.shape["svoc"]),
        ("dp", "tvoc_0", "tvoc_1", "svoc"),
    )
    placed = (
        P("dp", TVOC),
        P(TVOC, "svoc", None, None, None),
        P(TVOC, "svoc", None, None),
        P(TVOC, "svoc"),
        P("dp", None),
        P(None, TVOC_SVOC),
    )
    return jax.shard_map(
        local,
        mesh=finer,
        in_specs=placed,
        out_specs=(P("dp"), P("dp", TVOC_SVOC), P("dp", TVOC_SVOC)),
        check_vma=False,
    )
```

```python
import jax
import jax.numpy as jnp
from jax import lax
from jax.experimental import pallas as pl
from jax.experimental.pallas import tpu as pltpu
from jax.sharding import Mesh
from jax.sharding import PartitionSpec as P

CAP = 2
TVOC = ("tvoc_0", "tvoc_1")
TVOC_SVOC = ("tvoc_0", "tvoc_1", "svoc")
LOSS_SCALE = 128.0
F32 = jnp.float32
BF16 = jnp.bfloat16
EXTRA = 8
FIRST_OWNER = 10
FIRST_SVOC = 4


def vmem():
    return pl.BlockSpec(memory_space=pltpu.VMEM)


def hbm():
    return pl.BlockSpec(memory_space=pltpu.HBM)


def params(limit=20):
    return pltpu.CompilerParams(vmem_limit_bytes=limit << 20)


def as_row(tile):
    return jnp.sum(tile.T, axis=0, keepdims=True)


def turned(length, first):
    return [(k + first) % length for k in range(length)]


def lane_blocks(array, width=128):
    return [array[:, k : k + width] for k in range(0, array.shape[1], width)]


def in_parts(row):
    high = row.astype(BF16)
    rest = row - high.astype(F32)
    middle = rest.astype(BF16)
    low = (rest - middle.astype(F32)).astype(BF16)
    return high.astype(F32), middle.astype(F32), low.astype(F32)


def rows_of(parts, height, width):
    at = lax.broadcasted_iota(jnp.int32, (height, width), 0)
    out = jnp.zeros((height, width), F32)
    for k, part in enumerate(parts):
        out = jnp.where(at == k, part, out)
    return out


def stats_kernel(
    slots, w_parts,
    index_h, count_h, probs_h, values_h, hidden_h, weight_h,
    logits_h, stats,
    index, count, probs, values, hidden, weight, logits, sems,
):
    blk = values.shape[-1]
    depth = weight.shape[0] // w_parts
    small = [
        pltpu.make_async_copy(index_h, index, sems.at[3 + w_parts]),
        pltpu.make_async_copy(count_h, count, sems.at[4 + w_parts]),
    ]
    copies = [
        pltpu.make_async_copy(values_h, values, sems.at[0]),
        pltpu.make_async_copy(probs_h, probs, sems.at[1]),
        pltpu.make_async_copy(hidden_h, hidden, sems.at[2]),
    ] + [
        pltpu.make_async_copy(
            weight_h.at[pl.ds(k * depth, depth)], weight.at[pl.ds(k * depth, depth)], sems.at[3 + k]
        )
        for k in range(w_parts)
    ]
    for copy in small + copies:
        copy.start()
    for copy in small:
        copy.wait()
    live_slots = count[0, 0]
    copies[0].wait()
    copies[1].wait()
    mass = jnp.zeros((probs.shape[0], blk), F32)
    for s in range(slots):
        live = s < live_slots
        at = pl.multiple_of(jnp.where(live, index[0, s], 0) * blk, blk)
        block = jnp.dot(probs[:, pl.ds(at, blk)], values[s], preferred_element_type=F32)
        mass = mass + jnp.where(live, block, 0.0)
    mass_row = as_row(mass)
    copies[2].wait()
    total = jnp.zeros(logits.shape, F32)
    for k in range(w_parts):
        copies[3 + k].wait()
        total = total + jnp.dot(
            hidden[:, k * depth : (k + 1) * depth],
            weight[k * depth : (k + 1) * depth, :],
            preferred_element_type=F32,
        )
    logits[...] = total
    leaving = pltpu.make_async_copy(logits, logits_h, sems.at[5 + w_parts])
    leaving.start()
    parts = lane_blocks(total)
    top = parts[0]
    for part in parts[1:]:
        top = jnp.maximum(top, part)
    largest = jnp.max(top, axis=1, keepdims=True)
    sums = sum(jnp.exp(part - largest) for part in parts)
    largest_row = jnp.max(top.T, axis=0, keepdims=True)
    lse = largest_row + jnp.log(as_row(sums))
    both = jnp.concatenate([lse, mass_row], axis=0)
    stats[...] = jnp.broadcast_to(both[None], stats.shape)
    leaving.wait()


def mapping_kernel(
    slots, owners, per_owner,
    index_h, count_h, probs_h, values_h,
    outgoing,
    index, count, probs, values, mapped, first, second, place, sems,
):
    blk = values.shape[-1]
    small = [
        pltpu.make_async_copy(index_h, index, sems.at[2]),
        pltpu.make_async_copy(count_h, count, sems.at[3]),
    ]
    copies = [
        pltpu.make_async_copy(values_h, values, sems.at[0]),
        pltpu.make_async_copy(probs_h, probs, sems.at[1]),
    ]
    for copy in small + copies:
        copy.start()
    for o in range(owners):
        first[o] = -1
        second[o] = -1
    for copy in small:
        copy.wait()
    live_slots = count[0, 0]
    for s in range(slots):
        live = s < live_slots
        column = jnp.where(live, index[1, s], 0)
        owner = column // per_owner
        had = first[owner]
        other = jnp.logical_and(had >= 0, had != column)
        first[owner] = jnp.where(jnp.logical_and(live, had < 0), column, had)
        second[owner] = jnp.where(jnp.logical_and(live, other), column, second[owner])
        place[s] = jnp.where(live, owner * CAP + jnp.where(other, 1, 0), owners * CAP)
    mapped[...] = jnp.zeros_like(mapped)
    for copy in copies:
        copy.wait()
    for s in range(slots):
        row = jnp.where(s < live_slots, index[0, s], 0)
        at = pl.multiple_of(row * blk, blk)
        block = jnp.dot(probs[:, pl.ds(at, blk)], values[s], preferred_element_type=F32)
        mapped[place[s]] += block
    for k, o in enumerate(turned(owners, FIRST_OWNER)):
        for c in range(CAP):
            outgoing[k, c * blk : (c + 1) * blk, :] = mapped[o * CAP + c].astype(BF16)
        label_a = lax.rem(jnp.maximum(first[o], 0), per_owner).astype(F32)
        label_b = lax.rem(jnp.maximum(second[o], 0), per_owner).astype(F32)
        at = lax.broadcasted_iota(jnp.int32, (EXTRA, blk), 0)
        outgoing[k, CAP * blk :, :] = jnp.where(
            at == 0, label_a, jnp.where(at == 1, label_b, 0.0)
        ).astype(BF16)


def combined(lses, masses):
    top = jnp.max(lses, axis=0, keepdims=True)
    lse = top + jnp.log(jnp.sum(jnp.exp(lses - top), axis=0, keepdims=True))
    return lse, jnp.sum(masses, axis=0, keepdims=True)


def tail_kernel(stats, _, outgoing, tails, sems):
    there = outgoing.at[:, pl.ds(CAP * tails.shape[2], EXTRA), :]
    labels = pltpu.make_async_copy(there, tails, sems.at[0])
    labels.start()
    count = stats.shape[0]
    lse, mass = combined(
        jnp.concatenate([stats[k, 0:1, :] for k in range(count)], axis=0),
        jnp.concatenate([stats[k, 1:2, :] for k in range(count)], axis=0),
    )
    added = rows_of([0.0, 0.0, *in_parts(lse), *in_parts(mass)], EXTRA, lse.shape[1])
    labels.wait()
    for o in range(tails.shape[0]):
        tails[o] = (tails[o].astype(F32) + added).astype(BF16)
    copy = pltpu.make_async_copy(tails, there, sems.at[1])
    copy.start()
    copy.wait()


def middle_kernel(per_owner, chunks, received, logits, weight, grad, outgoing, finals):
    sources = received.shape[0]
    blk = received.shape[2]
    tails = [received[s, CAP * blk :, :].astype(F32) for s in range(sources)]
    lse, mass_sum = combined(
        jnp.concatenate([jnp.sum(t[2:5], axis=0, keepdims=True) for t in tails], axis=0),
        jnp.concatenate([jnp.sum(t[5:8], axis=0, keepdims=True) for t in tails], axis=0),
    )
    finals[...] = lse
    lse_column = jnp.broadcast_to(lse, (blk, blk)).T
    scale = jnp.broadcast_to(LOSS_SCALE / mass_sum, (blk, blk)).T
    spread = jnp.zeros(scale.shape, F32)
    masses = [jnp.zeros(scale.shape, F32) for _ in range(per_owner)]
    for s in range(sources):
        for c in range(CAP):
            label = tails[s][c : c + 1, :]
            piece = received[s, c * blk : (c + 1) * blk, :].astype(F32)
            for b in range(per_owner):
                masses[b] = masses[b] + jnp.where(label == float(b), piece, 0.0)
    for b in range(per_owner):
        at = slice(b * blk, (b + 1) * blk)
        mass = masses[b]
        positive = mass > 0
        spread = spread + jnp.where(
            positive, mass * (jnp.log(jnp.where(positive, mass, 1.0)) - logits[:, at]), 0.0
        )
        soft = LOSS_SCALE * jnp.exp(logits[:, at] - lse_column)
        grad[:, at] = (soft - mass * scale).astype(BF16)
    sums = [*in_parts(as_row(spread)), *in_parts(as_row(sum(masses[1:], masses[0])))]
    tail = rows_of(sums, EXTRA, blk).astype(BF16)
    owners, height = outgoing.shape[0], outgoing.shape[1] - EXTRA
    step = owners // chunks
    place = turned(owners, owners - FIRST_OWNER)
    grads = grad[...]
    for k in range(chunks):
        rows = lax.dot_general(
            weight[k * step * height : (k + 1) * step * height, :], grads,
            (((1,), (1,)), ((), ())), preferred_element_type=F32,
        ).astype(BF16)
        for o in range(step):
            at = place[k * step + o]
            outgoing[at, :height, :] = rows[o * height : (o + 1) * height]
            outgoing[at, height:, :] = tail


def head_kernel(mine, other, grad_mine, grad_other, out):
    dims = (((0,), (0,)), ((), ()))
    out[...] = (
        lax.dot_general(mine[...], grad_mine[...], dims, preferred_element_type=F32)
        + lax.dot_general(other[...], grad_other[...], dims, preferred_element_type=F32)
    ).astype(BF16)


def half_sum_kernel(received, outgoing):
    total = received[0].astype(F32)
    for s in range(1, received.shape[0]):
        total = total + received[s].astype(F32)
    owners, height = outgoing.shape[0], outgoing.shape[1] - EXTRA
    sums = [
        part
        for at in (owners * height, owners * height + 3)
        for part in in_parts(jnp.sum(total[at : at + 3], axis=0, keepdims=True))
    ]
    tail = rows_of(sums, EXTRA, total.shape[1]).astype(BF16)
    for k, o in enumerate(turned(owners, FIRST_SVOC)):
        outgoing[k, :height, :] = total[o * height : (o + 1) * height].astype(BF16)
        outgoing[k, height:, :] = tail


def last_sum_kernel(received, finals, divergence, grad_hidden):
    total = received[0].astype(F32)
    for s in range(1, received.shape[0]):
        total = total + received[s].astype(F32)
    height = grad_hidden.shape[0]
    grad_hidden[...] = total[:height]
    spread = jnp.sum(total[height : height + 3], axis=0, keepdims=True)
    mass = jnp.sum(total[height + 3 : height + 6], axis=0, keepdims=True)
    divergence[...] = spread / mass - jnp.log(mass) + finals[...]


def local(teacher_probs, block_values, block_index, block_count, hidden, student_weight):
    tokens, width = hidden.shape
    slots, blk = block_values.shape[2], block_values.shape[-1]
    owners, svocs = lax.axis_size(TVOC), lax.axis_size("svoc")
    shard = student_weight.shape[1]
    per_owner = shard // blk
    shape = jax.ShapeDtypeStruct
    w_parts = 6
    half = width // lax.axis_size("dp")
    me = lax.axis_index("dp")
    swap = [(0, 1), (1, 0)]
    tvoc_order = [turned(owners, FIRST_OWNER)]
    svoc_order = [turned(svocs, FIRST_SVOC)]
    hidden_mine = lax.dynamic_slice_in_dim(hidden, me * half, half, 1)
    hidden_other = lax.ppermute(
        lax.dynamic_slice_in_dim(hidden, (1 - me) * half, half, 1), "dp", swap
    )

    index, values = block_index[0, 0].T, block_values[0, 0]

    def stats_of(*refs):
        stats_kernel(slots, w_parts, *refs)

    logits, stats = pl.pallas_call(
        stats_of,
        out_shape=(shape((tokens, shard), F32), shape((svocs, 2, tokens), F32)),
        in_specs=[hbm()] * 6,
        out_specs=(hbm(), vmem()),
        scratch_shapes=[
            pltpu.SMEM(index.shape, jnp.int32),
            pltpu.SMEM(block_count.shape, jnp.int32),
            pltpu.VMEM(teacher_probs.shape, BF16),
            pltpu.VMEM(values.shape, BF16),
            pltpu.VMEM(hidden.shape, BF16),
            pltpu.VMEM(student_weight.shape, BF16),
            pltpu.VMEM((tokens, shard), F32),
            pltpu.SemaphoreType.DMA((6 + w_parts,)),
        ],
        compiler_params=params(60),
        name="stats",
    )(index, block_count, teacher_probs, values, hidden, student_weight)
    near_stats = lax.all_to_all(stats, "svoc", 0, 0, tiled=True, axis_index_groups=svoc_order)

    def mapping(*refs):
        mapping_kernel(slots, owners, per_owner, *refs)

    outgoing = pl.pallas_call(
        mapping,
        out_shape=shape((owners, CAP * blk + EXTRA, blk), BF16),
        in_specs=[hbm()] * 4,
        out_specs=vmem(),
        scratch_shapes=[
            pltpu.SMEM(index.shape, jnp.int32),
            pltpu.SMEM(block_count.shape, jnp.int32),
            pltpu.VMEM(teacher_probs.shape, BF16),
            pltpu.VMEM(values.shape, BF16),
            pltpu.VMEM((owners * CAP + 1, tokens, blk), F32),
            pltpu.SMEM((owners,), jnp.int32),
            pltpu.SMEM((owners,), jnp.int32),
            pltpu.SMEM((slots,), jnp.int32),
            pltpu.SemaphoreType.DMA((4,)),
        ],
        compiler_params=params(),
        cost_estimate=pl.CostEstimate(
            flops=2 * slots * tokens * blk * blk, bytes_accessed=4 << 20, transcendentals=0
        ),
        name="mapping",
    )(index, block_count, teacher_probs, values)
    outgoing = pl.pallas_call(
        tail_kernel,
        out_shape=shape(outgoing.shape, BF16),
        in_specs=[vmem(), hbm()],
        out_specs=hbm(),
        scratch_shapes=[pltpu.VMEM((owners, EXTRA, blk), BF16), pltpu.SemaphoreType.DMA((2,))],
        input_output_aliases={1: 0},
        compiler_params=params(),
        name="tail",
    )(near_stats, outgoing)
    received = lax.all_to_all(outgoing, TVOC, 0, 0, tiled=True, axis_index_groups=tvoc_order)
    height = width // owners

    def middle(*refs):
        middle_kernel(per_owner, 4, *refs)

    grad, partial_hidden, finals = pl.pallas_call(
        middle,
        out_shape=(
            shape((tokens, shard), BF16),
            shape((owners, height + EXTRA, tokens), BF16),
            shape((1, tokens), F32),
        ),
        in_specs=[vmem()] * 3,
        out_specs=(vmem(),) * 3,
        compiler_params=params(),
        name="middle",
    )(received, logits, student_weight)
    grad_other = lax.ppermute(grad, "dp", swap)
    summed = lax.all_to_all(
        partial_hidden, TVOC, 0, 0, tiled=True, axis_index_groups=tvoc_order
    )
    tiles = 4
    grad_weight = pl.pallas_call(
        head_kernel,
        out_shape=shape((half, shard), BF16),
        grid=(tiles,),
        in_specs=[
            pl.BlockSpec((tokens, half // tiles), lambda i: (0, i)),
            pl.BlockSpec((tokens, half // tiles), lambda i: (0, i)),
            pl.BlockSpec((tokens, shard), lambda i: (0, 0)),
            pl.BlockSpec((tokens, shard), lambda i: (0, 0)),
        ],
        out_specs=pl.BlockSpec((half // tiles, shard), lambda i: (i, 0)),
        compiler_params=params(),
        name="head",
    )(hidden_mine, hidden_other, grad, grad_other)
    last = height // svocs
    summed, grad_weight = lax.optimization_barrier((summed, grad_weight))
    nearer = pl.pallas_call(
        half_sum_kernel,
        out_shape=shape((svocs, last + EXTRA, tokens), BF16),
        in_specs=[vmem()],
        out_specs=vmem(),
        compiler_params=params(),
        name="half_sum",
    )(summed)
    arrived = lax.all_to_all(nearer, "svoc", 0, 0, tiled=True, axis_index_groups=svoc_order)
    divergence, grad_hidden = pl.pallas_call(
        last_sum_kernel,
        out_shape=(shape((1, tokens), F32), shape((last, tokens), F32)),
        in_specs=[vmem()] * 2,
        out_specs=(vmem(),) * 2,
        compiler_params=params(),
        name="last_sum",
    )(arrived, finals)
    return (divergence[0], grad_weight, grad_hidden.T)


def solution(mesh):
    finer = Mesh(
        mesh.devices.reshape(mesh.shape["dp"], 4, 4, mesh.shape["svoc"]),
        ("dp", "tvoc_0", "tvoc_1", "svoc"),
    )
    placed = (
        P("dp", TVOC),
        P(TVOC, "svoc", None, None, None),
        P(TVOC, "svoc", None, None),
        P(TVOC, "svoc"),
        P("dp", None),
        P(None, TVOC_SVOC),
    )
    return jax.shard_map(
        local,
        mesh=finer,
        in_specs=placed,
        out_specs=(P("dp"), P("dp", TVOC_SVOC), P("dp", TVOC_SVOC)),
        check_vma=False,
    )
```

```python
import jax
import jax.numpy as jnp
from jax import lax
from jax.experimental import pallas as pl
from jax.experimental.pallas import tpu as pltpu
from jax.sharding import Mesh
from jax.sharding import PartitionSpec as P

CAP = 2
TVOC = ("tvoc_0", "tvoc_1")
TVOC_SVOC = ("tvoc_0", "tvoc_1", "svoc")
LOSS_SCALE = 128.0
F32 = jnp.float32
BF16 = jnp.bfloat16
EXTRA = 8
FIRST_OWNER = 10
SVOC_ORDER = [4, 0, 7, 1, 6, 2, 5, 3]


def vmem():
    return pl.BlockSpec(memory_space=pltpu.VMEM)


def hbm():
    return pl.BlockSpec(memory_space=pltpu.HBM)


def params(limit=20):
    return pltpu.CompilerParams(vmem_limit_bytes=limit << 20)


def as_row(tile):
    return jnp.sum(tile.T, axis=0, keepdims=True)


def turned(length, first):
    return [(k + first) % length for k in range(length)]


def lane_blocks(array, width=128):
    return [array[:, k : k + width] for k in range(0, array.shape[1], width)]


def in_parts(row):
    high = row.astype(BF16)
    rest = row - high.astype(F32)
    middle = rest.astype(BF16)
    low = (rest - middle.astype(F32)).astype(BF16)
    return high.astype(F32), middle.astype(F32), low.astype(F32)


def rows_of(parts, height, width):
    at = lax.broadcasted_iota(jnp.int32, (height, width), 0)
    out = jnp.zeros((height, width), F32)
    for k, part in enumerate(parts):
        out = jnp.where(at == k, part, out)
    return out


def stats_kernel(
    slots, w_parts,
    index_h, count_h, probs_h, values_h, hidden_h, weight_h,
    logits_h, stats,
    index, count, probs, values, hidden, weight, logits, sems,
):
    blk = values.shape[-1]
    depth = weight.shape[0] // w_parts
    small = [
        pltpu.make_async_copy(index_h, index, sems.at[3 + w_parts]),
        pltpu.make_async_copy(count_h, count, sems.at[4 + w_parts]),
    ]
    copies = [
        pltpu.make_async_copy(values_h, values, sems.at[0]),
        pltpu.make_async_copy(probs_h, probs, sems.at[1]),
        pltpu.make_async_copy(hidden_h, hidden, sems.at[2]),
    ] + [
        pltpu.make_async_copy(
            weight_h.at[pl.ds(k * depth, depth)], weight.at[pl.ds(k * depth, depth)], sems.at[3 + k]
        )
        for k in range(w_parts)
    ]
    for copy in small + copies:
        copy.start()
    for copy in small:
        copy.wait()
    live_slots = count[0, 0]
    copies[0].wait()
    copies[1].wait()
    mass = jnp.zeros((probs.shape[0], blk), F32)
    for s in range(slots):
        live = s < live_slots
        at = pl.multiple_of(jnp.where(live, index[0, s], 0) * blk, blk)
        block = jnp.dot(probs[:, pl.ds(at, blk)], values[s], preferred_element_type=F32)
        mass = mass + jnp.where(live, block, 0.0)
    mass_row = as_row(mass)
    copies[2].wait()
    total = jnp.zeros(logits.shape, F32)
    for k in range(w_parts):
        copies[3 + k].wait()
        total = total + jnp.dot(
            hidden[:, k * depth : (k + 1) * depth],
            weight[k * depth : (k + 1) * depth, :],
            preferred_element_type=F32,
        )
    logits[...] = total
    leaving = pltpu.make_async_copy(logits, logits_h, sems.at[5 + w_parts])
    leaving.start()
    parts = lane_blocks(total)
    top = parts[0]
    for part in parts[1:]:
        top = jnp.maximum(top, part)
    largest = jnp.max(top, axis=1, keepdims=True)
    sums = sum(jnp.exp(part - largest) for part in parts)
    largest_row = jnp.max(top.T, axis=0, keepdims=True)
    lse = largest_row + jnp.log(as_row(sums))
    both = jnp.concatenate([lse, mass_row], axis=0)
    stats[...] = jnp.broadcast_to(both[None], stats.shape)
    leaving.wait()


def mapping_kernel(
    slots, owners, per_owner,
    index_h, count_h, probs_h, values_h,
    outgoing,
    index, count, probs, values, mapped, first, second, place, sems,
):
    blk = values.shape[-1]
    small = [
        pltpu.make_async_copy(index_h, index, sems.at[2]),
        pltpu.make_async_copy(count_h, count, sems.at[3]),
    ]
    copies = [
        pltpu.make_async_copy(values_h, values, sems.at[0]),
        pltpu.make_async_copy(probs_h, probs, sems.at[1]),
    ]
    for copy in small + copies:
        copy.start()
    for o in range(owners):
        first[o] = -1
        second[o] = -1
    for copy in small:
        copy.wait()
    live_slots = count[0, 0]
    for s in range(slots):
        live = s < live_slots
        column = jnp.where(live, index[1, s], 0)
        owner = column // per_owner
        had = first[owner]
        other = jnp.logical_and(had >= 0, had != column)
        first[owner] = jnp.where(jnp.logical_and(live, had < 0), column, had)
        second[owner] = jnp.where(jnp.logical_and(live, other), column, second[owner])
        place[s] = jnp.where(live, owner * CAP + jnp.where(other, 1, 0), owners * CAP)
    mapped[...] = jnp.zeros_like(mapped)
    for copy in copies:
        copy.wait()
    for s in range(slots):
        row = jnp.where(s < live_slots, index[0, s], 0)
        at = pl.multiple_of(row * blk, blk)
        block = jnp.dot(probs[:, pl.ds(at, blk)], values[s], preferred_element_type=F32)
        mapped[place[s]] += block
    for k, o in enumerate(turned(owners, FIRST_OWNER)):
        for c in range(CAP):
            outgoing[k, c * blk : (c + 1) * blk, :] = mapped[o * CAP + c].astype(BF16)
        label_a = lax.rem(jnp.maximum(first[o], 0), per_owner).astype(F32)
        label_b = lax.rem(jnp.maximum(second[o], 0), per_owner).astype(F32)
        at = lax.broadcasted_iota(jnp.int32, (EXTRA, blk), 0)
        outgoing[k, CAP * blk :, :] = jnp.where(
            at == 0, label_a, jnp.where(at == 1, label_b, 0.0)
        ).astype(BF16)


def combined(lses, masses):
    top = jnp.max(lses, axis=0, keepdims=True)
    lse = top + jnp.log(jnp.sum(jnp.exp(lses - top), axis=0, keepdims=True))
    return lse, jnp.sum(masses, axis=0, keepdims=True)


def tail_kernel(stats, _, outgoing, tails, sems):
    there = outgoing.at[:, pl.ds(CAP * tails.shape[2], EXTRA), :]
    labels = pltpu.make_async_copy(there, tails, sems.at[0])
    labels.start()
    count = stats.shape[0]
    lse, mass = combined(
        jnp.concatenate([stats[k, 0:1, :] for k in range(count)], axis=0),
        jnp.concatenate([stats[k, 1:2, :] for k in range(count)], axis=0),
    )
    added = rows_of([0.0, 0.0, *in_parts(lse), *in_parts(mass)], EXTRA, lse.shape[1])
    labels.wait()
    for o in range(tails.shape[0]):
        tails[o] = (tails[o].astype(F32) + added).astype(BF16)
    copy = pltpu.make_async_copy(tails, there, sems.at[1])
    copy.start()
    copy.wait()


def middle_kernel(per_owner, chunks, received, logits, weight, grad, outgoing, finals):
    sources = received.shape[0]
    blk = received.shape[2]
    tails = [received[s, CAP * blk :, :].astype(F32) for s in range(sources)]
    lse, mass_sum = combined(
        jnp.concatenate([jnp.sum(t[2:5], axis=0, keepdims=True) for t in tails], axis=0),
        jnp.concatenate([jnp.sum(t[5:8], axis=0, keepdims=True) for t in tails], axis=0),
    )
    finals[...] = lse
    lse_column = jnp.broadcast_to(lse, (blk, blk)).T
    scale = jnp.broadcast_to(LOSS_SCALE / mass_sum, (blk, blk)).T
    spread = jnp.zeros(scale.shape, F32)
    masses = [jnp.zeros(scale.shape, F32) for _ in range(per_owner)]
    for s in range(sources):
        for c in range(CAP):
            label = tails[s][c : c + 1, :]
            piece = received[s, c * blk : (c + 1) * blk, :].astype(F32)
            for b in range(per_owner):
                masses[b] = masses[b] + jnp.where(label == float(b), piece, 0.0)
    for b in range(per_owner):
        at = slice(b * blk, (b + 1) * blk)
        mass = masses[b]
        positive = mass > 0
        spread = spread + jnp.where(
            positive, mass * (jnp.log(jnp.where(positive, mass, 1.0)) - logits[:, at]), 0.0
        )
        soft = LOSS_SCALE * jnp.exp(logits[:, at] - lse_column)
        grad[:, at] = (soft - mass * scale).astype(BF16)
    sums = [*in_parts(as_row(spread)), *in_parts(as_row(sum(masses[1:], masses[0])))]
    tail = rows_of(sums, EXTRA, blk).astype(BF16)
    owners, height = outgoing.shape[0], outgoing.shape[1] - EXTRA
    step = owners // chunks
    place = turned(owners, owners - FIRST_OWNER)
    grads = grad[...]
    for k in range(chunks):
        rows = lax.dot_general(
            weight[k * step * height : (k + 1) * step * height, :], grads,
            (((1,), (1,)), ((), ())), preferred_element_type=F32,
        ).astype(BF16)
        for o in range(step):
            at = place[k * step + o]
            outgoing[at, :height, :] = rows[o * height : (o + 1) * height]
            outgoing[at, height:, :] = tail


def head_kernel(mine, other, grad_mine, grad_other, out):
    dims = (((0,), (0,)), ((), ()))
    out[...] = (
        lax.dot_general(mine[...], grad_mine[...], dims, preferred_element_type=F32)
        + lax.dot_general(other[...], grad_other[...], dims, preferred_element_type=F32)
    ).astype(BF16)


def half_sum_kernel(received, outgoing):
    total = received[0].astype(F32)
    for s in range(1, received.shape[0]):
        total = total + received[s].astype(F32)
    owners, height = outgoing.shape[0], outgoing.shape[1] - EXTRA
    sums = [
        part
        for at in (owners * height, owners * height + 3)
        for part in in_parts(jnp.sum(total[at : at + 3], axis=0, keepdims=True))
    ]
    tail = rows_of(sums, EXTRA, total.shape[1]).astype(BF16)
    for k, o in enumerate(SVOC_ORDER):
        outgoing[k, :height, :] = total[o * height : (o + 1) * height].astype(BF16)
        outgoing[k, height:, :] = tail


def last_sum_kernel(received, finals, divergence, grad_hidden):
    total = received[0].astype(F32)
    for s in range(1, received.shape[0]):
        total = total + received[s].astype(F32)
    height = grad_hidden.shape[0]
    grad_hidden[...] = total[:height]
    spread = jnp.sum(total[height : height + 3], axis=0, keepdims=True)
    mass = jnp.sum(total[height + 3 : height + 6], axis=0, keepdims=True)
    divergence[...] = spread / mass - jnp.log(mass) + finals[...]


def local(teacher_probs, block_values, block_index, block_count, hidden, student_weight):
    tokens, width = hidden.shape
    slots, blk = block_values.shape[2], block_values.shape[-1]
    owners, svocs = lax.axis_size(TVOC), lax.axis_size("svoc")
    assert svocs == len(SVOC_ORDER)
    shard = student_weight.shape[1]
    per_owner = shard // blk
    shape = jax.ShapeDtypeStruct
    w_parts = 6
    half = width // lax.axis_size("dp")
    me = lax.axis_index("dp")
    swap = [(0, 1), (1, 0)]
    tvoc_order = [turned(owners, FIRST_OWNER)]
    svoc_order = [SVOC_ORDER]
    hidden_mine = lax.dynamic_slice_in_dim(hidden, me * half, half, 1)
    hidden_other = lax.ppermute(
        lax.dynamic_slice_in_dim(hidden, (1 - me) * half, half, 1), "dp", swap
    )

    index, values = block_index[0, 0].T, block_values[0, 0]

    def stats_of(*refs):
        stats_kernel(slots, w_parts, *refs)

    logits, stats = pl.pallas_call(
        stats_of,
        out_shape=(shape((tokens, shard), F32), shape((svocs, 2, tokens), F32)),
        in_specs=[hbm()] * 6,
        out_specs=(hbm(), vmem()),
        scratch_shapes=[
            pltpu.SMEM(index.shape, jnp.int32),
            pltpu.SMEM(block_count.shape, jnp.int32),
            pltpu.VMEM(teacher_probs.shape, BF16),
            pltpu.VMEM(values.shape, BF16),
            pltpu.VMEM(hidden.shape, BF16),
            pltpu.VMEM(student_weight.shape, BF16),
            pltpu.VMEM((tokens, shard), F32),
            pltpu.SemaphoreType.DMA((6 + w_parts,)),
        ],
        compiler_params=params(60),
        name="stats",
    )(index, block_count, teacher_probs, values, hidden, student_weight)
    near_stats = lax.all_to_all(stats, "svoc", 0, 0, tiled=True, axis_index_groups=svoc_order)

    def mapping(*refs):
        mapping_kernel(slots, owners, per_owner, *refs)

    outgoing = pl.pallas_call(
        mapping,
        out_shape=shape((owners, CAP * blk + EXTRA, blk), BF16),
        in_specs=[hbm()] * 4,
        out_specs=vmem(),
        scratch_shapes=[
            pltpu.SMEM(index.shape, jnp.int32),
            pltpu.SMEM(block_count.shape, jnp.int32),
            pltpu.VMEM(teacher_probs.shape, BF16),
            pltpu.VMEM(values.shape, BF16),
            pltpu.VMEM((owners * CAP + 1, tokens, blk), F32),
            pltpu.SMEM((owners,), jnp.int32),
            pltpu.SMEM((owners,), jnp.int32),
            pltpu.SMEM((slots,), jnp.int32),
            pltpu.SemaphoreType.DMA((4,)),
        ],
        compiler_params=params(),
        cost_estimate=pl.CostEstimate(
            flops=2 * slots * tokens * blk * blk, bytes_accessed=4 << 20, transcendentals=0
        ),
        name="mapping",
    )(index, block_count, teacher_probs, values)
    outgoing = pl.pallas_call(
        tail_kernel,
        out_shape=shape(outgoing.shape, BF16),
        in_specs=[vmem(), hbm()],
        out_specs=hbm(),
        scratch_shapes=[pltpu.VMEM((owners, EXTRA, blk), BF16), pltpu.SemaphoreType.DMA((2,))],
        input_output_aliases={1: 0},
        compiler_params=params(),
        name="tail",
    )(near_stats, outgoing)
    received = lax.all_to_all(outgoing, TVOC, 0, 0, tiled=True, axis_index_groups=tvoc_order)
    height = width // owners

    def middle(*refs):
        middle_kernel(per_owner, 4, *refs)

    grad, partial_hidden, finals = pl.pallas_call(
        middle,
        out_shape=(
            shape((tokens, shard), BF16),
            shape((owners, height + EXTRA, tokens), BF16),
            shape((1, tokens), F32),
        ),
        in_specs=[vmem()] * 3,
        out_specs=(vmem(),) * 3,
        compiler_params=params(),
        name="middle",
    )(received, logits, student_weight)
    grad_other = lax.ppermute(grad, "dp", swap)
    summed = lax.all_to_all(
        partial_hidden, TVOC, 0, 0, tiled=True, axis_index_groups=tvoc_order
    )
    tiles = 2
    grad_weight = pl.pallas_call(
        head_kernel,
        out_shape=shape((half, shard), BF16),
        grid=(tiles,),
        in_specs=[
            pl.BlockSpec((tokens, half // tiles), lambda i: (0, i)),
            pl.BlockSpec((tokens, half // tiles), lambda i: (0, i)),
            pl.BlockSpec((tokens, shard), lambda i: (0, 0)),
            pl.BlockSpec((tokens, shard), lambda i: (0, 0)),
        ],
        out_specs=pl.BlockSpec((half // tiles, shard), lambda i: (i, 0)),
        compiler_params=params(),
        name="head",
    )(hidden_mine, hidden_other, grad, grad_other)
    last = height // svocs
    summed, grad_weight = lax.optimization_barrier((summed, grad_weight))
    nearer = pl.pallas_call(
        half_sum_kernel,
        out_shape=shape((svocs, last + EXTRA, tokens), BF16),
        in_specs=[vmem()],
        out_specs=vmem(),
        compiler_params=params(),
        name="half_sum",
    )(summed)
    arrived = lax.all_to_all(nearer, "svoc", 0, 0, tiled=True, axis_index_groups=svoc_order)
    divergence, grad_hidden = pl.pallas_call(
        last_sum_kernel,
        out_shape=(shape((1, tokens), F32), shape((last, tokens), F32)),
        in_specs=[vmem()] * 2,
        out_specs=(vmem(),) * 2,
        compiler_params=params(),
        name="last_sum",
    )(arrived, finals)
    return (divergence[0], grad_weight, grad_hidden.T)


def solution(mesh):
    finer = Mesh(
        mesh.devices.reshape(mesh.shape["dp"], 4, 4, mesh.shape["svoc"]),
        ("dp", "tvoc_0", "tvoc_1", "svoc"),
    )
    placed = (
        P("dp", TVOC),
        P(TVOC, "svoc", None, None, None),
        P(TVOC, "svoc", None, None),
        P(TVOC, "svoc"),
        P("dp", None),
        P(None, TVOC_SVOC),
    )
    return jax.shard_map(
        local,
        mesh=finer,
        in_specs=placed,
        out_specs=(P("dp"), P("dp", TVOC_SVOC), P("dp", TVOC_SVOC)),
        check_vma=False,
    )
```
